256 devices in a mesh: outer: 16 (over x, z_hi), inner: 16 (over z_lo, y, core).
Axes of the slice: x: 4, y: 4, z: 8 (z_hi: 4, z_lo: 2; z = z_hi * 2 + z_lo), core: 2. Of those that a mesh axis runs over, the one named last changes fastest.
Arguments:
- query_in: bfloat16 [32768, 1024], P(('outer', 'inner')), may hold values from -6 to 6
- key_in: bfloat16 [32768, 1024], P(('outer', 'inner')), may hold values from -6 to 6
- value_in: bfloat16 [32768, 1024], P(('outer', 'inner')), may hold values from -6 to 6
- conv_taps: float32 [3, 3, 1024], replicated, may hold values from -3.5 to 3.5
- long_filter: float32 [32768, 1024], P(('outer', 'inner')), may hold values from -1.1 to 1.1
- skip_gain: float32 [1024], replicated, may hold values from 0.5 to 1.5
- grad_out: bfloat16 [32768, 1024], P(('outer', 'inner')), may hold values from -6 to 6
Outputs:
- output: bfloat16 [32768, 1024], P(('outer', 'inner'))
- grad_query: bfloat16 [32768, 1024], P(('outer', 'inner'))
- grad_key: bfloat16 [32768, 1024], P(('outer', 'inner'))
- grad_value: bfloat16 [32768, 1024], P(('outer', 'inner'))
The draws below stay inside these ranges and needn't reach their ends.
All inputs are finite; a program needn't handle non-finite values.
Results may differ from the reference program's by a relative error of at most 0.001.
Values may be sent and summed in bfloat16 or wider, within the bound.
A program may use at most 64 MiB of HBM per device.

```python
import math
import jax
import jax.numpy as jnp

CH = 1024
SEQ = 32768


def draw_long_filter(key, part):
    subkeys = jax.random.split(key, 4)
    position = jnp.arange(SEQ, dtype=jnp.int32)[:, None]
    distance = position.astype(jnp.float32)
    reaches = jnp.exp(jax.random.uniform(subkeys[0], (CH,), jnp.float32, math.log(30.0), math.log(4.0 * SEQ)))
    roughness = jnp.clip(jax.random.normal(subkeys[1], (SEQ, CH), jnp.float32), -4.0, 4.0)
    drop_places = jax.random.randint(subkeys[2], (3, CH), 0, SEQ)
    drop_sizes = jax.random.uniform(subkeys[3], (3, CH), jnp.float32, 0.5, 0.8)
    envelope = jnp.exp(-distance / reaches)
    for which_drop in range(3):
        envelope = envelope * jnp.where(position >= drop_places[which_drop], drop_sizes[which_drop], 1.0)
    normalizer = jnp.sqrt(2.0 / (reaches * (1.0 - jnp.exp(-2.0 * SEQ / reaches))))
    return roughness * envelope * normalizer


def level_of(stream_key, shape, cuts, smallest, top_value):
    level, own = 1.0, jax.random.fold_in(stream_key, 6)
    for axis_at, blocks in cuts:
        heights = jnp.exp(jax.random.uniform(jax.random.fold_in(own, axis_at), (blocks,), jnp.float32, smallest / len(cuts), top_value / len(cuts)))
        level = level * jnp.repeat(heights, shape[axis_at] // blocks).reshape([-1 if axis == axis_at else 1 for axis in range(len(shape))])
    return level


def bell_draw(rng, dims, spread, reach, cuts=(), held_as=jnp.bfloat16):
    values = spread * jax.random.normal(rng, dims, jnp.float32)
    if cuts:
        values = values * level_of(rng, dims, cuts, -0.22, 0.18)
    return jnp.clip(values, -reach, reach).astype(held_as)


def setup_inputs(seed: int = 0) -> dict:
    key_of = jax.random.split(jax.random.key(seed), 8)
    query_in = bell_draw(key_of[0], (SEQ, CH), 1.0, 6.0, ((0, 256),))
    key_in = bell_draw(key_of[1], (SEQ, CH), 1.0, 6.0, ((0, 256),))
    value_in = bell_draw(key_of[2], (SEQ, CH), 1.0, 6.0, ((0, 256),))
    conv_taps = bell_draw(key_of[3], (3, 3, CH), 3 ** -0.5, 3.5, (), jnp.float32)
    long_filter = draw_long_filter(jax.random.fold_in(key_of[7], 71), 0)
    skip_gain = jnp.clip(jax.random.uniform(key_of[5], (CH,), jnp.float32, 0.5, 1.5), 0.5, 1.5)
    grad_out = bell_draw(key_of[6], (SEQ, CH), 1.0, 6.0, ((0, 256),))
    return {"query_in": query_in, "key_in": key_in, "value_in": value_in, "conv_taps": conv_taps, "long_filter": long_filter, "skip_gain": skip_gain, "grad_out": grad_out}


def short_forward(stream, tap_set):
    padded = jnp.pad(stream, ((2, 0), (0, 0)))
    return tap_set[0] * stream + tap_set[1] * padded[1:-1] + tap_set[2] * padded[:-2]


def short_backward(grad_rows, tap_set):
    padded = jnp.pad(grad_rows, ((0, 2), (0, 0)))
    return tap_set[0] * grad_rows + tap_set[1] * padded[1:-1] + tap_set[2] * padded[2:]


def reference(query_in, key_in, value_in, conv_taps, long_filter, skip_gain, grad_out):
    length = query_in.shape[0]
    points = 2 * length
    short_q = short_forward(query_in.astype(jnp.float32), conv_taps[0])
    short_k = short_forward(key_in.astype(jnp.float32), conv_taps[1])
    short_v = short_forward(value_in.astype(jnp.float32), conv_taps[2])
    gated = short_k * short_v
    spec_filter = jnp.fft.rfft(long_filter, n=points, axis=0)
    spec_gated = jnp.fft.rfft(gated, n=points, axis=0)
    convolved = jnp.fft.irfft(spec_gated * spec_filter, n=points, axis=0)[:length]
    mixed = convolved + skip_gain * gated
    output = (short_q * mixed).astype(jnp.bfloat16)
    upstream = grad_out.astype(jnp.float32)
    grad_short_q = upstream * mixed
    grad_mixed = upstream * short_q
    spec_grad = jnp.fft.rfft(grad_mixed, n=points, axis=0)
    grad_gated = jnp.fft.irfft(jnp.conj(spec_filter) * spec_grad, n=points, axis=0)[:length] + skip_gain * grad_mixed
    grad_short_k = grad_gated * short_v
    grad_short_v = grad_gated * short_k
    grad_query = short_backward(grad_short_q, conv_taps[0]).astype(jnp.bfloat16)
    grad_key = short_backward(grad_short_k, conv_taps[1]).astype(jnp.bfloat16)
    grad_value = short_backward(grad_short_v, conv_taps[2]).astype(jnp.bfloat16)
    return (output, grad_query, grad_key, grad_value)
```

```python
import functools

import jax
import jax.numpy as jnp
import numpy as np
from jax import lax
from jax.experimental import pallas as pl
from jax.experimental.pallas import tpu as pltpu
from jax.sharding import PartitionSpec as P

MESH = pl.DeviceIdType.MESH
F32, BF16 = jnp.float32, jnp.bfloat16
X, Z, Y, C = 4, 8, 4, 2
W = X * Y * C
D = 256
T = 128
POINTS = 2 * D * T


def dft_constants():
    k = np.arange(D)[:, None] + 0.5
    d = np.arange(D)[None, :]
    coarse = 2 * np.pi * (k * d / (2 * D) % 1.0)
    forward = np.concatenate([np.cos(coarse), -np.sin(coarse)], 0)
    backward = np.concatenate([np.cos(coarse).T, -np.sin(coarse).T], 1) * (2.0 / POINTS)
    t = np.arange(T)[None, :]
    turn = 2 * np.pi * (k * t / POINTS % 1.0)
    fine = 2 * np.pi * (t.T * t % T) / T
    c, s = np.cos(fine), np.sin(fine)
    fine_forward = np.block([[c, -s], [s, c]])
    fine_backward = np.block([[c, s], [-s, c]])

    def halves(m):
        m = m.astype(np.float32)
        high = m.astype(jnp.bfloat16)
        low = (m - high.astype(np.float32)).astype(jnp.bfloat16)
        return np.stack([high, low])

    fine_both = np.stack([halves(fine_forward), halves(fine_backward)])
    twist = np.stack([np.cos(turn), np.sin(turn)]).astype(np.float32)
    return halves(forward), halves(backward), fine_both, twist


def place():
    o, i = lax.axis_index("outer"), lax.axis_index("inner")
    return o // 4, (o % 4) * 2 + i // 8, i % 8


def device(x, z, yc):
    return (x * 4 + z // 2, (z % 2) * 8 + yc)


def halves_of(v):
    high = v.astype(BF16)
    return high, (v - high.astype(F32)).astype(BF16)


def dot(a, b):
    return jnp.dot(a, b, preferred_element_type=F32)


def choose_matrix():
    r = lax.broadcasted_iota(jnp.int32, (256, 256), 0)
    c = lax.broadcasted_iota(jnp.int32, (256, 256), 1)
    wanted = ((r // 4) % 2) * 128 + (r // 8) * 4 + r % 4
    return jnp.where(c == wanted, 1.0, 0.0).astype(BF16)


def main_kernel(
    q_hbm, k_hbm, v_hbm, g_hbm, f_hbm, taps, skip, fwd_hbm, bwd_hbm, fine_hbm, twist_hbm,
    back,
    kin, vin, qin, gin, fin, fwd, bwd, fine, twist,
    choose, snd, mid, rcv, rows, spec, coarse, work, gated, mixed, grad, streams, osnd, omid,
    in_sem, local_sem, zs_sem, zr_sem, xs_sem, xr_sem,
):
    x, z, yc = place()
    w = x * 8 + yc

    loads = [
        pltpu.make_async_copy(a, b, in_sem.at[n])
        for n, (a, b) in enumerate(
            [(f_hbm, fin), (k_hbm, kin), (v_hbm, vin), (q_hbm, qin), (g_hbm, gin),
             (fwd_hbm, fwd), (fine_hbm, fine), (twist_hbm, twist), (bwd_hbm, bwd)]
        )
    ]
    for load in loads:
        load.start()

    barrier = pltpu.get_barrier_semaphore()

    def greet_z(i, _):
        pl.semaphore_signal(barrier, inc=1, device_id=device(x, (z + i) % Z, yc), device_id_type=MESH)
        return 0

    def greet_w(i, _):
        there = (w + i) % W
        pl.semaphore_signal(barrier, inc=1, device_id=device(there // 8, z, there % 8), device_id_type=MESH)
        return 0

    lax.fori_loop(1, Z, greet_z, 0)
    lax.fori_loop(1, W, greet_w, 0)
    choose[...] = choose_matrix()

    def pack(p, left, right):
        def block(b, _):
            cols = pl.ds(pl.multiple_of(b * 128, 128), 128)
            pair = jnp.concatenate([left(cols), right(cols)], axis=1)
            turned = lax.dot_general(
                choose[...], pair, (((1,), (1,)), ((), ())), preferred_element_type=F32
            )
            snd[p, b] = turned.reshape(W, 8, T).astype(BF16)
            return 0

        lax.fori_loop(0, Z, block, 0)

    def send_z(p, source, target):
        def one(i, _):
            s, dz = i // 7, i % 7 + 1
            zt = (z + dz) % Z
            pltpu.make_async_remote_copy(
                src_ref=source(zt, s), dst_ref=target(s),
                send_sem=zs_sem.at[p], recv_sem=zr_sem.at[p, s],
                device_id=device(x, zt, yc), device_id_type=MESH,
            ).start()
            return 0

        lax.fori_loop(0, X * (Z - 1), one, 0)
        for s in range(X):
            pltpu.make_async_copy(source(z, s), target(s), local_sem.at[p, s]).start()

    def forward(p, s, middle, target, own):
        part = middle.at[pl.ds(s * 8, 8), z]
        pltpu.make_async_copy(part, part, local_sem.at[p, s]).wait()
        arrived = middle.at[pl.ds(s * 8, 8), pl.ds(0, Z - 1)]
        pltpu.make_async_remote_copy(
            src_ref=arrived, dst_ref=arrived, send_sem=zs_sem.at[p], recv_sem=zr_sem.at[p, s],
            device_id=device(x, z, yc), device_id_type=MESH,
        ).wait_recv()

        def one(i, _):
            there = (yc + i) % 8
            @pl.when(jnp.logical_or(s != x, i != 0))
            def _():
                pltpu.make_async_remote_copy(
                    src_ref=middle.at[s * 8 + there], dst_ref=target,
                    send_sem=xs_sem.at[p], recv_sem=xr_sem.at[p],
                    device_id=device(s, z, there), device_id_type=MESH,
                ).start()
            return 0

        lax.fori_loop(0, 8, one, 0)

    def await_all(p, middle, target):
        own = pltpu.make_async_copy(middle.at[w], target, local_sem.at[p, X])
        own.start()
        own.wait()
        part = middle.at[pl.ds(0, W - 1)]
        pltpu.make_async_remote_copy(
            src_ref=part, dst_ref=part, send_sem=xs_sem.at[p], recv_sem=xr_sem.at[p],
            device_id=device(x, z, yc), device_id_type=MESH,
        ).wait_recv()

    def in_target(p):
        return rcv.at[p, x, :, yc]

    def in_send(p):
        send_z(
            p,
            lambda zt, s: snd.at[p, zt, pl.ds(s * 8, 8)],
            lambda s: mid.at[p, pl.ds(s * 8, 8), z],
        )

    def in_forward(p, s):
        forward(p, s, mid.at[p], in_target(p), None)

    def in_await(p):
        await_all(p, mid.at[p], in_target(p))
        for b in range(X):
            rows[pl.ds(b * 512, 512)] = rcv[p, b].astype(F32).reshape(512, T)

    def row(r):
        return rows[pl.ds(r, D, stride=8), :]

    loads[0].wait()

    def filter_high(cols):
        return fin[:, cols].astype(BF16)

    def filter_low(cols):
        value = fin[:, cols]
        return (value - value.astype(BF16).astype(F32)).astype(BF16)

    pack(0, filter_high, filter_low)
    pl.semaphore_wait(barrier, Z + W - 2)
    in_send(0)
    loads[1].wait()
    loads[2].wait()
    pack(1, lambda cols: kin[:, cols], lambda cols: vin[:, cols])
    in_send(1)
    loads[3].wait()
    loads[4].wait()
    pack(2, lambda cols: qin[:, cols], lambda cols: gin[:, cols])
    in_send(2)
    for load in loads[5:]:
        load.wait()

    lane = lax.broadcasted_iota(jnp.int32, (D, T), 1)
    block_row = lax.broadcasted_iota(jnp.int32, (D, T), 0)

    def delayed(v, n):
        turned = pltpu.roll(v, n, axis=1)
        before = jnp.where(block_row == 0, 0.0, pltpu.roll(turned, 1, axis=0))
        return jnp.where(lane < n, before, turned)

    def advanced(v, n):
        turned = pltpu.roll(v, T - n, axis=1)
        after = jnp.where(block_row == D - 1, 0.0, pltpu.roll(turned, D - 1, axis=0))
        return jnp.where(lane >= T - n, after, turned)

    first_channel = 4 * (z * W + w)

    def short_forward(v, stream, j):
        tap = [taps[stream, n, first_channel + j] for n in range(3)]
        return tap[0] * v + tap[1] * delayed(v, 1) + tap[2] * delayed(v, 2)

    def short_backward(v, stream, j):
        tap = [taps[stream, n, first_channel + j] for n in range(3)]
        return tap[0] * v + tap[1] * advanced(v, 1) + tap[2] * advanced(v, 2)

    def put_columns(v, at):
        high, low = halves_of(v)
        work[0, 0:D, pl.ds(at * T, T)] = high
        work[1, 0:D, pl.ds(at * T, T)] = low

    def transform(out, pair):
        for b in range(2):
            part = pl.ds(b * D, D)
            high = work[0, 0:D]
            coarse[part] = (
                dot(fwd[0, part], high) + dot(fwd[1, part], high) + dot(fwd[0, part], work[1, 0:D])
            )
        tc, ts = twist[0], twist[1]
        for n in range(2):
            cols = pl.ds(n * T, T)
            re, im = coarse[0:D, cols], coarse[D : 2 * D, cols]
            both = jnp.concatenate([re * tc + im * ts, im * tc - re * ts], axis=1)
            high, low = halves_of(both)
            out[2 * pair + n] = (
                dot(high, fine[0, 0]) + dot(low, fine[0, 0]) + dot(high, fine[0, 1])
            )

    def untransform(left, right, conjugate, out, pair):
        tc, ts = twist[0], twist[1]
        for n in range(2):
            a, b = left[2 * pair + n], right[2 * pair + n]
            ar, ai, br, bi = a[:, 0:T], a[:, T:], b[:, 0:T], b[:, T:]
            if conjugate:
                re, im = ar * br + ai * bi, ar * bi - ai * br
            else:
                re, im = ar * br - ai * bi, ar * bi + ai * br
            high, low = halves_of(jnp.concatenate([re, im], axis=1))
            back_spec = dot(high, fine[1, 0]) + dot(low, fine[1, 0]) + dot(high, fine[1, 1])
            gr, gi = back_spec[:, 0:T], back_spec[:, T:]
            cols = pl.ds(n * T, T)
            high, low = halves_of(gr * tc - gi * ts)
            work[0, 0:D, cols] = high
            work[1, 0:D, cols] = low
            high, low = halves_of(gi * tc + gr * ts)
            work[0, D : 2 * D, cols] = high
            work[1, D : 2 * D, cols] = low
        result = dot(bwd[0], work[0]) + dot(bwd[1], work[0]) + dot(bwd[0], work[1])
        for n in range(2):
            out[2 * pair + n] = result[:, n * T : n * T + T]

    for s in range(X):
        in_forward(0, s)
    in_await(0)

    def filter_pair(pair, _):
        in_forward(1, pair)
        for n in range(2):
            work[0, 0:D, pl.ds(n * T, T)] = row(2 * pair + n).astype(BF16)
            work[1, 0:D, pl.ds(n * T, T)] = row(2 * pair + n + 4).astype(BF16)
        transform(spec.at[0], pair)
        return 0

    lax.fori_loop(0, 2, filter_pair, 0)
    in_forward(1, 2)
    in_forward(1, 3)
    in_await(1)

    def gated_pair(pair, _):
        in_forward(2, pair)
        for n in range(2):
            j = 2 * pair + n
            short_k = short_forward(row(j), 1, j)
            short_v = short_forward(row(j + 4), 2, j)
            streams[0, j] = short_k
            streams[1, j] = short_v
            value = short_k * short_v
            gated[j] = value
            put_columns(value, n)
        transform(spec.at[1], pair)
        untransform(spec.at[1], spec.at[0], False, mixed, pair)
        for n in range(2):
            j = 2 * pair + n
            mixed[j] = mixed[j] + skip[first_channel + j] * gated[j]
        return 0

    lax.fori_loop(0, 2, gated_pair, 0)
    in_forward(2, 2)
    in_forward(2, 3)
    in_await(2)

    def query_channel(j, _):
        short_q = short_forward(row(j), 0, j)
        upstream = row(j + 4)
        grad[j] = upstream * short_q
        rows[pl.ds(j, D, stride=8), :] = short_q * mixed[j]
        rows[pl.ds(j + 4, D, stride=8), :] = short_backward(upstream * mixed[j], 0, j)
        return 0

    lax.fori_loop(0, 4, query_channel, 0)

    def out_send(p):
        for b in range(X):
            osnd[p, b] = rows[pl.ds(b * 512, 512)].reshape(Z, 8, 8, T).astype(BF16)
        send_z(
            p + 3,
            lambda zt, s: osnd.at[p, s, zt],
            lambda s: omid.at[p, pl.ds(s * 8, 8), z],
        )

    def out_target(p):
        return back.at[p, :, w]

    def out_forward(p, s):
        forward(p + 3, s, omid.at[p], out_target(p), None)

    out_send(0)

    def grad_pair(pair, _):
        for n in range(2):
            put_columns(grad[2 * pair + n], n)
        transform(spec.at[1], pair)
        out_forward(0, 2 * pair)
        untransform(spec.at[0], spec.at[1], True, mixed, pair)
        for n in range(2):
            j = 2 * pair + n
            total = mixed[j] + skip[first_channel + j] * grad[j]
            rows[pl.ds(j, D, stride=8), :] = short_backward(total * streams[1, j], 1, j)
            rows[pl.ds(j + 4, D, stride=8), :] = short_backward(total * streams[0, j], 2, j)
        out_forward(0, 2 * pair + 1)
        return 0

    lax.fori_loop(0, 2, grad_pair, 0)
    out_send(1)
    for s in range(X):
        out_forward(1, s)
    for p in range(2):
        await_all(p + 3, omid.at[p], out_target(p))
    for p in range(5):
        sent = mid.at[0, pl.ds(0, W - 1)]
        pltpu.make_async_remote_copy(
            src_ref=sent, dst_ref=sent, send_sem=xs_sem.at[p], recv_sem=xr_sem.at[p],
            device_id=device(x, z, yc), device_id_type=MESH,
        ).wait_send()
        sent = snd.at[0, pl.ds(0, Z - 1)]
        pltpu.make_async_remote_copy(
            src_ref=sent, dst_ref=sent, send_sem=zs_sem.at[p], recv_sem=zr_sem.at[p, 0],
            device_id=device(x, z, yc), device_id_type=MESH,
        ).wait_send()


def finish_kernel(back, out_a, out_b, out_c, out_d):
    choose = choose_matrix()
    for p, pair in enumerate(((out_a, out_b), (out_c, out_d))):
        for b in range(Z):
            turned = lax.dot_general(
                back[p, b].reshape(256, T), choose, (((0,), (0,)), ((), ())), preferred_element_type=F32
            ).astype(BF16)
            for n in range(2):
                pair[n][:, b * 128 : b * 128 + 128] = turned[:, n * 128 : n * 128 + 128]


def local(query_in, key_in, value_in, conv_taps, long_filter, skip_gain, grad_out):
    forward, backward, fine, twist = (jnp.asarray(m) for m in dft_constants())
    anywhere = pl.BlockSpec(memory_space=pl.ANY)
    scalars = pl.BlockSpec(memory_space=pltpu.SMEM)
    vmem = pl.BlockSpec(memory_space=pltpu.VMEM)
    tokens = pltpu.VMEM((T, 1024), BF16)
    back = pl.pallas_call(
        main_kernel,
        out_shape=jax.ShapeDtypeStruct((2, Z, W, 8, T), BF16),
        in_specs=[anywhere] * 5 + [scalars] * 2 + [anywhere] * 4,
        out_specs=vmem,
        scratch_shapes=[
            tokens, tokens, tokens, tokens,
            pltpu.VMEM((T, 1024), F32),
            pltpu.VMEM(forward.shape, BF16),
            pltpu.VMEM(backward.shape, BF16),
            pltpu.VMEM(fine.shape, BF16),
            pltpu.VMEM(twist.shape, F32),
            pltpu.VMEM((256, 256), BF16),
            pltpu.VMEM((3, Z, W, 8, T), BF16),
            pltpu.VMEM((3, W, Z, 8, T), BF16),
            pltpu.VMEM((3, X, Z, 8, 8, T), BF16),
            pltpu.VMEM((2048, T), F32),
            pltpu.VMEM((2, 4, D, 2 * T), F32),
            pltpu.VMEM((2 * D, 2 * T), F32),
            pltpu.VMEM((2, 2 * D, 2 * T), BF16),
            pltpu.VMEM((4, D, T), F32),
            pltpu.VMEM((4, D, T), F32),
            pltpu.VMEM((4, D, T), F32),
            pltpu.VMEM((2, 4, D, T), F32),
            pltpu.VMEM((2, X, Z, 8, 8, T), BF16),
            pltpu.VMEM((2, W, Z, 8, T), BF16),
            pltpu.SemaphoreType.DMA((9,)),
            pltpu.SemaphoreType.DMA((5, X + 1)),
            pltpu.SemaphoreType.DMA((5,)),
            pltpu.SemaphoreType.DMA((5, X)),
            pltpu.SemaphoreType.DMA((5,)),
            pltpu.SemaphoreType.DMA((5,)),
        ],
        compiler_params=pltpu.CompilerParams(
            collective_id=0, has_side_effects=True, vmem_limit_bytes=40 << 20
        ),
        name="hyena_exchange",
    )(query_in, key_in, value_in, grad_out, long_filter, conv_taps, skip_gain, forward, backward, fine, twist)
    result = jax.ShapeDtypeStruct((T, 1024), BF16)
    return tuple(
        pl.pallas_call(
            finish_kernel,
            out_shape=(result,) * 4,
            in_specs=[vmem],
            out_specs=(vmem,) * 4,
            name="hyena_finish",
        )(back)
    )


def solution(mesh):
    tokens = P(("outer", "inner"), None)
    return jax.shard_map(
        local,
        mesh=mesh,
        in_specs=(tokens, tokens, tokens, P(), tokens, P(), tokens),
        out_specs=(tokens,) * 4,
        check_vma=False,
    )
```

```python
import functools

import jax
import jax.numpy as jnp
import numpy as np
from jax import lax
from jax.experimental import pallas as pl
from jax.experimental.pallas import tpu as pltpu
from jax.sharding import PartitionSpec as P

MESH = pl.DeviceIdType.MESH
F32, BF16 = jnp.float32, jnp.bfloat16
X, Z, Y, C = 4, 8, 4, 2
W = X * Y * C
D = 256
T = 128
POINTS = 2 * D * T


def dft_constants():
    k = np.arange(D)[:, None] + 0.5
    d = np.arange(D)[None, :]
    coarse = 2 * np.pi * (k * d / (2 * D) % 1.0)
    forward = np.concatenate([np.cos(coarse), -np.sin(coarse)], 0)
    backward = np.concatenate([np.cos(coarse).T, -np.sin(coarse).T], 1) * (2.0 / POINTS)
    t = np.arange(T)[None, :]
    turn = 2 * np.pi * (k * t / POINTS % 1.0)
    fine = 2 * np.pi * (t.T * t % T) / T
    c, s = np.cos(fine), np.sin(fine)
    fine_forward = np.block([[c, -s], [s, c]])
    fine_backward = np.block([[c, s], [-s, c]])

    def halves(m):
        m = m.astype(np.float32)
        high = m.astype(jnp.bfloat16)
        low = (m - high.astype(np.float32)).astype(jnp.bfloat16)
        return np.stack([high, low])

    fine_both = np.stack([halves(fine_forward), halves(fine_backward)])
    twist = np.stack([np.cos(turn), np.sin(turn)]).astype(np.float32)
    return halves(forward), halves(backward), fine_both, twist


def place():
    o, i = lax.axis_index("outer"), lax.axis_index("inner")
    return o // 4, (o % 4) * 2 + i // 8, i % 8


def device(x, z, yc):
    return (x * 4 + z // 2, (z % 2) * 8 + yc)


def halves_of(v):
    high = v.astype(BF16)
    return high, (v - high.astype(F32)).astype(BF16)


def dot(a, b):
    return jnp.dot(a, b, preferred_element_type=F32)


def identity():
    r = lax.broadcasted_iota(jnp.int32, (256, 256), 0)
    c = lax.broadcasted_iota(jnp.int32, (256, 256), 1)
    return jnp.where(r == c, 1.0, 0.0).astype(BF16)


K_IN, V_IN, F_HIGH, F_LOW, Q_IN, G_IN, OUT, GRAD_Q, GRAD_K, GRAD_V = range(10)
FINE_PARTS = (G_IN, GRAD_V)
ORDER = (2, 1, 3, 0)


def main_kernel(
    q_hbm, k_hbm, v_hbm, g_hbm, f_hbm, taps, skip, fwd_hbm, bwd_hbm, fine_hbm, twist_hbm,
    back,
    kin, vin, qin, gin, fin, fwd, bwd, fine, twist,
    eye, snd, mid, rcv, rows, spec, coarse, work, gated, mixed, grad, streams, osnd,
    in_sem, local_sem, zs_sem, zr_sem, xs_sem, xr_sem,
):
    x, z, yc = place()
    w = x * 8 + yc

    loads = [
        pltpu.make_async_copy(a, b, in_sem.at[n])
        for n, (a, b) in enumerate(
            [(k_hbm, kin), (v_hbm, vin), (f_hbm, fin), (q_hbm, qin), (g_hbm, gin),
             (fwd_hbm, fwd), (fine_hbm, fine), (twist_hbm, twist), (bwd_hbm, bwd)]
        )
    ]
    for load in loads:
        load.start()

    barrier = pltpu.get_barrier_semaphore()

    def greet_z(i, _):
        pl.semaphore_signal(barrier, inc=1, device_id=device(x, (z + i) % Z, yc), device_id_type=MESH)
        return 0

    def greet_w(i, _):
        there = (w + i) % W
        pl.semaphore_signal(barrier, inc=1, device_id=device(there // 8, z, there % 8), device_id_type=MESH)
        return 0

    lax.fori_loop(1, Z, greet_z, 0)
    lax.fori_loop(1, W, greet_w, 0)
    eye[...] = identity()

    def pack(p, value):
        def block(b, _):
            cols = pl.ds(pl.multiple_of(b * 256, 256), 256)
            turned = lax.dot_general(
                eye[...], value(cols), (((1,), (1,)), ((), ())), preferred_element_type=F32
            )
            snd[p, pl.ds(b * 2, 2)] = turned.reshape(2, W, 4, T).astype(BF16)
            return 0

        lax.fori_loop(0, Z // 2, block, 0)

    def groups_of(p):
        if p in FINE_PARTS:
            return [(n, ((x + dx) % X) * 8, 8) for n, dx in enumerate(ORDER)]
        return [(0, 0, W)]

    def send_z(p, source):
        for n, first, count in groups_of(p):
            def one(dz, _):
                zt = (z + dz) % Z
                pltpu.make_async_remote_copy(
                    src_ref=source(zt, first, count), dst_ref=mid.at[p, pl.ds(first, count), z],
                    send_sem=zs_sem.at[p], recv_sem=zr_sem.at[p, n],
                    device_id=device(x, zt, yc), device_id_type=MESH,
                ).start()
                return 0

            lax.fori_loop(1, Z, one, 0)
            pltpu.make_async_copy(
                source(z, first, count), mid.at[p, pl.ds(first, count), z], local_sem.at[p, n]
            ).start()

    def target_of(p):
        if p < OUT:
            return rcv.at[p, x, :, yc]
        return back.at[p - OUT, :, w]

    def forward(p, group):
        n, first, count = groups_of(p)[group]
        part = mid.at[p, pl.ds(first, count), z]
        pltpu.make_async_copy(part, part, local_sem.at[p, n]).wait()
        arrived = mid.at[p, pl.ds(first, count), pl.ds(0, Z - 1)]
        pltpu.make_async_remote_copy(
            src_ref=arrived, dst_ref=arrived, send_sem=zs_sem.at[p], recv_sem=zr_sem.at[p, n],
            device_id=device(x, z, yc), device_id_type=MESH,
        ).wait_recv()
        target = target_of(p)

        def one_of(dx):
            def one(i, _):
                xt, there = (x + dx) % X, (yc + i) % 8
                pltpu.make_async_remote_copy(
                    src_ref=mid.at[p, xt * 8 + there], dst_ref=target,
                    send_sem=xs_sem.at[p], recv_sem=xr_sem.at[p],
                    device_id=device(xt, z, there), device_id_type=MESH,
                ).start()
                return 0

            return one

        for dx in [ORDER[group]] if p in FINE_PARTS else ORDER:
            lax.fori_loop(1 if dx == 0 else 0, 8, one_of(dx), 0)
            if dx == 0:
                pltpu.make_async_copy(mid.at[p, w], target, local_sem.at[p, X]).start()

    def await_all(p):
        pltpu.make_async_copy(mid.at[p, w], target_of(p), local_sem.at[p, X]).wait()
        part = mid.at[p, pl.ds(0, W - 1)]
        pltpu.make_async_remote_copy(
            src_ref=part, dst_ref=part, send_sem=xs_sem.at[p], recv_sem=xr_sem.at[p],
            device_id=device(x, z, yc), device_id_type=MESH,
        ).wait_recv()

    def unpack(p, slot):
        await_all(p)
        for b in range(X):
            rows[slot, pl.ds(b * 256, 256)] = rcv[p, b].astype(F32).reshape(256, T)

    def row(slot, j):
        return rows[slot, pl.ds(j, D, stride=4), :]

    def put_row(slot, j, value):
        rows[slot, pl.ds(j, D, stride=4), :] = value

    def in_send(p):
        send_z(p, lambda zt, first, count: snd.at[p, zt, pl.ds(first, count)])

    def out_send(p, slot):
        for b in range(X):
            osnd[p - OUT, pl.ds(b * 8, 8)] = (
                rows[slot, pl.ds(b * 256, 256)].reshape(Z, 8, 4, T).swapaxes(0, 1).astype(BF16)
            )
        send_z(p, lambda zt, first, count: osnd.at[p - OUT, pl.ds(first, count), zt])

    def filter_high(cols):
        return fin[:, cols].astype(BF16)

    def filter_low(cols):
        value = fin[:, cols]
        return (value - value.astype(BF16).astype(F32)).astype(BF16)

    loads[0].wait()
    pack(K_IN, lambda cols: kin[:, cols])
    pl.semaphore_wait(barrier, Z + W - 2)
    in_send(K_IN)
    loads[1].wait()
    pack(V_IN, lambda cols: vin[:, cols])
    in_send(V_IN)
    loads[2].wait()
    pack(F_HIGH, filter_high)
    in_send(F_HIGH)
    pack(F_LOW, filter_low)
    in_send(F_LOW)
    loads[3].wait()
    pack(Q_IN, lambda cols: qin[:, cols])
    in_send(Q_IN)
    loads[4].wait()
    pack(G_IN, lambda cols: gin[:, cols])
    in_send(G_IN)
    for load in loads[5:]:
        load.wait()

    lane = lax.broadcasted_iota(jnp.int32, (D, T), 1)
    block_row = lax.broadcasted_iota(jnp.int32, (D, T), 0)

    def delayed(v, n):
        turned = pltpu.roll(v, n, axis=1)
        before = jnp.where(block_row == 0, 0.0, pltpu.roll(turned, 1, axis=0))
        return jnp.where(lane < n, before, turned)

    def advanced(v, n):
        turned = pltpu.roll(v, T - n, axis=1)
        after = jnp.where(block_row == D - 1, 0.0, pltpu.roll(turned, D - 1, axis=0))
        return jnp.where(lane >= T - n, after, turned)

    first_channel = 4 * (z * W + w)

    def short_forward(v, stream, j):
        tap = [taps[stream, n, first_channel + j] for n in range(3)]
        return tap[0] * v + tap[1] * delayed(v, 1) + tap[2] * delayed(v, 2)

    def short_backward(v, stream, j):
        tap = [taps[stream, n, first_channel + j] for n in range(3)]
        return tap[0] * v + tap[1] * advanced(v, 1) + tap[2] * advanced(v, 2)

    def put_columns(v, at):
        high, low = halves_of(v)
        work[0, 0:D, pl.ds(at * T, T)] = high
        work[1, 0:D, pl.ds(at * T, T)] = low

    def transform(out, pair):
        for b in range(2):
            part = pl.ds(b * D, D)
            high = work[0, 0:D]
            coarse[part] = (
                dot(fwd[0, part], high) + dot(fwd[1, part], high) + dot(fwd[0, part], work[1, 0:D])
            )
        tc, ts = twist[0], twist[1]
        for n in range(2):
            cols = pl.ds(n * T, T)
            re, im = coarse[0:D, cols], coarse[D : 2 * D, cols]
            both = jnp.concatenate([re * tc + im * ts, im * tc - re * ts], axis=1)
            high, low = halves_of(both)
            out[2 * pair + n] = (
                dot(high, fine[0, 0]) + dot(low, fine[0, 0]) + dot(high, fine[0, 1])
            )

    def untransform(left, right, conjugate, out, pair):
        tc, ts = twist[0], twist[1]
        for n in range(2):
            a, b = left[2 * pair + n], right[2 * pair + n]
            ar, ai, br, bi = a[:, 0:T], a[:, T:], b[:, 0:T], b[:, T:]
            if conjugate:
                re, im = ar * br + ai * bi, ar * bi - ai * br
            else:
                re, im = ar * br - ai * bi, ar * bi + ai * br
            high, low = halves_of(jnp.concatenate([re, im], axis=1))
            back_spec = dot(high, fine[1, 0]) + dot(low, fine[1, 0]) + dot(high, fine[1, 1])
            gr, gi = back_spec[:, 0:T], back_spec[:, T:]
            cols = pl.ds(n * T, T)
            high, low = halves_of(gr * tc - gi * ts)
            work[0, 0:D, cols] = high
            work[1, 0:D, cols] = low
            high, low = halves_of(gi * tc + gr * ts)
            work[0, D : 2 * D, cols] = high
            work[1, D : 2 * D, cols] = low
        result = dot(bwd[0], work[0]) + dot(bwd[1], work[0]) + dot(bwd[0], work[1])
        for n in range(2):
            out[2 * pair + n] = result[:, n * T : n * T + T]

    def each(count, body):
        def step(i, _):
            body(i)
            return 0

        lax.fori_loop(0, count, step, 0)

    def key_channel(j):
        streams[0, j] = short_forward(row(0, j), 1, j)

    def value_channel(j):
        short_v = short_forward(row(1, j), 2, j)
        streams[1, j] = short_v
        gated[j] = streams[0, j] * short_v

    def gated_pair(pair):
        for n in range(2):
            put_columns(gated[2 * pair + n], n)
        transform(spec.at[1], pair)

    def filter_pair(pair):
        for n in range(2):
            work[0, 0:D, pl.ds(n * T, T)] = row(0, 2 * pair + n).astype(BF16)
            work[1, 0:D, pl.ds(n * T, T)] = row(1, 2 * pair + n).astype(BF16)
        transform(spec.at[0], pair)
        untransform(spec.at[1], spec.at[0], False, mixed, pair)
        for n in range(2):
            j = 2 * pair + n
            mixed[j] = mixed[j] + skip[first_channel + j] * gated[j]

    def query_channel(j):
        short_q = short_forward(row(0, j), 0, j)
        grad[j] = short_q
        put_row(0, j, short_q * mixed[j])

    def upstream_channel(j):
        upstream = row(1, j)
        put_row(1, j, short_backward(upstream * mixed[j], 0, j))
        grad[j] = upstream * grad[j]

    def grad_pair(pair):
        for n in range(2):
            put_columns(grad[2 * pair + n], n)
        transform(spec.at[1], pair)
        untransform(spec.at[0], spec.at[1], True, mixed, pair)
        for n in range(2):
            j = 2 * pair + n
            total = mixed[j] + skip[first_channel + j] * grad[j]
            put_row(0, j, short_backward(total * streams[1, j], 1, j))
            put_row(1, j, short_backward(total * streams[0, j], 2, j))

    forward(K_IN, 0)
    forward(V_IN, 0)
    unpack(K_IN, 0)
    each(4, key_channel)
    unpack(V_IN, 1)
    each(4, value_channel)
    forward(F_HIGH, 0)
    each(2, gated_pair)
    forward(F_LOW, 0)
    unpack(F_HIGH, 0)
    unpack(F_LOW, 1)
    filter_pair(0)
    forward(Q_IN, 0)
    filter_pair(1)
    unpack(Q_IN, 0)
    each(4, query_channel)
    out_send(OUT, 0)
    for group in range(X):
        forward(G_IN, group)
    unpack(G_IN, 1)
    each(4, upstream_channel)
    out_send(GRAD_Q, 1)
    grad_pair(0)
    forward(OUT, 0)
    grad_pair(1)
    out_send(GRAD_K, 0)
    out_send(GRAD_V, 1)
    forward(GRAD_Q, 0)
    forward(GRAD_K, 0)
    for group in range(X):
        forward(GRAD_V, group)
    for p in range(OUT, 10):
        await_all(p)
    for p in range(10):
        sent = mid.at[p, pl.ds(0, W - 1)]
        pltpu.make_async_remote_copy(
            src_ref=sent, dst_ref=sent, send_sem=xs_sem.at[p], recv_sem=xr_sem.at[p],
            device_id=device(x, z, yc), device_id_type=MESH,
        ).wait_send()
        sent = mid.at[p, :, pl.ds(0, Z - 1)]
        pltpu.make_async_remote_copy(
            src_ref=sent, dst_ref=sent, send_sem=zs_sem.at[p], recv_sem=zr_sem.at[p, 0],
            device_id=device(x, z, yc), device_id_type=MESH,
        ).wait_send()


def finish_kernel(back, *outs):
    eye = identity()
    for p in range(4):
        outs[p][...] = lax.dot_general(
            back[p].reshape(256, T), eye, (((0,), (0,)), ((), ())), preferred_element_type=F32
        ).astype(BF16)


def local(query_in, key_in, value_in, conv_taps, long_filter, skip_gain, grad_out):
    forward, backward, fine, twist = (jnp.asarray(m) for m in dft_constants())
    anywhere = pl.BlockSpec(memory_space=pl.ANY)
    scalars = pl.BlockSpec(memory_space=pltpu.SMEM)
    tokens = pltpu.VMEM((T, 1024), BF16)
    back = pl.pallas_call(
        main_kernel,
        out_shape=jax.ShapeDtypeStruct((4, Z, W, 4, T), BF16),
        in_specs=[anywhere] * 5 + [scalars] * 2 + [anywhere] * 4,
        out_specs=pl.BlockSpec(memory_space=pltpu.HBM),
        scratch_shapes=[
            tokens, tokens, tokens, tokens,
            pltpu.VMEM((T, 1024), F32),
            pltpu.VMEM(forward.shape, BF16),
            pltpu.VMEM(backward.shape, BF16),
            pltpu.VMEM(fine.shape, BF16),
            pltpu.VMEM(twist.shape, F32),
            pltpu.VMEM((256, 256), BF16),
            pltpu.VMEM((6, Z, W, 4, T), BF16),
            pltpu.VMEM((10, W, Z, 4, T), BF16),
            pltpu.VMEM((6, X, Z, 8, 4, T), BF16),
            pltpu.VMEM((2, 4 * D, T), F32),
            pltpu.VMEM((2, 4, D, 2 * T), F32),
            pltpu.VMEM((2 * D, 2 * T), F32),
            pltpu.VMEM((2, 2 * D, 2 * T), BF16),
            pltpu.VMEM((4, D, T), F32),
            pltpu.VMEM((4, D, T), F32),
            pltpu.VMEM((4, D, T), F32),
            pltpu.VMEM((2, 4, D, T), F32),
            pltpu.VMEM((4, W, Z, 4, T), BF16),
            pltpu.SemaphoreType.DMA((9,)),
            pltpu.SemaphoreType.DMA((10, X + 1)),
            pltpu.SemaphoreType.DMA((10,)),
            pltpu.SemaphoreType.DMA((10, X)),
            pltpu.SemaphoreType.DMA((10,)),
            pltpu.SemaphoreType.DMA((10,)),
        ],
        compiler_params=pltpu.CompilerParams(
            collective_id=0, has_side_effects=True, vmem_limit_bytes=67043328
        ),
        name="hyena_exchange",
    )(query_in, key_in, value_in, grad_out, long_filter, conv_taps, skip_gain, forward, backward, fine, twist)
    result = jax.ShapeDtypeStruct((T, 1024), BF16)
    return tuple(
        pl.pallas_call(
            finish_kernel,
            out_shape=(result,) * 4,
            grid=(4,),
            in_specs=[pl.BlockSpec((4, 2, W, 4, T), lambda b: (0, b, 0, 0, 0))],
            out_specs=(pl.BlockSpec((T, 256), lambda b: (0, b)),) * 4,
            name="hyena_finish",
        )(back)
    )


def solution(mesh):
    tokens = P(("outer", "inner"), None)
    return jax.shard_map(
        local,
        mesh=mesh,
        in_specs=(tokens, tokens, tokens, P(), tokens, P(), tokens),
        out_specs=(tokens,) * 4,
        check_vma=False,
    )
```

```python
import functools

import jax
import jax.numpy as jnp
import numpy as np
from jax import lax
from jax.experimental import pallas as pl
from jax.experimental.pallas import tpu as pltpu
from jax.sharding import PartitionSpec as P

MESH = pl.DeviceIdType.MESH
F32, BF16 = jnp.float32, jnp.bfloat16
X, Z, Y, C = 4, 8, 4, 2
W = X * Y * C
D = 256
T = 128
POINTS = 2 * D * T


def dft_constants():
    k = np.arange(D)[:, None] + 0.5
    d = np.arange(D)[None, :]
    coarse = 2 * np.pi * (k * d / (2 * D) % 1.0)
    forward = np.concatenate([np.cos(coarse), -np.sin(coarse)], 0)
    backward = np.concatenate([np.cos(coarse).T, -np.sin(coarse).T], 1) * (2.0 / POINTS)
    t = np.arange(T)[None, :]
    turn = 2 * np.pi * (k * t / POINTS % 1.0)
    fine = 2 * np.pi * (t.T * t % T) / T
    c, s = np.cos(fine), np.sin(fine)
    fine_forward = np.block([[c, -s], [s, c]])
    fine_backward = np.block([[c, s], [-s, c]])

    def halves(m):
        m = m.astype(np.float32)
        high = m.astype(jnp.bfloat16)
        low = (m - high.astype(np.float32)).astype(jnp.bfloat16)
        return np.stack([high, low])

    fine_both = np.stack([halves(fine_forward), halves(fine_backward)])
    twist = np.stack([np.cos(turn), np.sin(turn)]).astype(np.float32)
    return halves(forward), halves(backward), fine_both, twist


def place():
    o, i = lax.axis_index("outer"), lax.axis_index("inner")
    return o // 4, (o % 4) * 2 + i // 8, i % 8


def device(x, z, yc):
    return (x * 4 + z // 2, (z % 2) * 8 + yc)


def halves_of(v):
    high = v.astype(BF16)
    return high, (v - high.astype(F32)).astype(BF16)


def dot(a, b):
    return jnp.dot(a, b, preferred_element_type=F32)


def identity():
    r = lax.broadcasted_iota(jnp.int32, (256, 256), 0)
    c = lax.broadcasted_iota(jnp.int32, (256, 256), 1)
    return jnp.where(r == c, 1.0, 0.0).astype(BF16)


FILTER, GATED, GRAD_MIXED, CONVOLVED, GRAD_GATED = range(5)
ORDER = (2, 1, 3, 0)
IN_SCALES, CONVOLVED_SCALE, GRAD_SCALE = range(3)

RATIO = 256.0
SHIFT = 124.0 * float(np.log(2.0))
SLOPE = 2.0 * SHIFT / float(np.log(1.0 + RATIO))
FILTER_TOP = 1.125


def encode(v, top):
    size = jnp.exp(SLOPE * jnp.log(1.0 + jnp.abs(v) * (RATIO / top)) - SHIFT)
    return jnp.where(v < 0.0, -size, size)


def decode(code, top):
    size = (jnp.exp((jnp.log(jnp.abs(code)) + SHIFT) * (1.0 / SLOPE)) - 1.0) * (top / RATIO)
    return jnp.where(code < 0.0, -size, size)


def main_kernel(
    q_hbm, k_hbm, v_hbm, g_hbm, f_hbm, taps, skip, fwd_hbm, bwd_hbm, fine_hbm, twist_hbm,
    out_ref, grad_q_ref, grad_k_ref, grad_v_ref,
    kin, vin, qin, gin, fin, fwd, bwd, fine, twist,
    eye, snd, mid, rcv, rows, spec, coarse, work, result, extended, short, gated, grad_mixed, tops,
    osnd, back, before, after, own_scale, mid_scale, in_scale, out_scale, scale_row,
    in_sem, local_sem, zs_sem, zr_sem, xs_sem, xr_sem, halo_s_sem, halo_r_sem,
    scale_local_sem, scale_zs_sem, scale_zr_sem, scale_xs_sem, scale_xr_sem,
):
    x, z, yc = place()
    w = x * 8 + yc
    d = x * 64 + z * 8 + yc
    next_d, last_d = (d + 1) % D, (d + D - 1) % D
    next_device = device(next_d // 64, (next_d // 8) % 8, next_d % 8)
    last_device = device(last_d // 64, (last_d // 8) % 8, last_d % 8)
    here = device(x, z, yc)

    loads = [
        pltpu.make_async_copy(a, b, in_sem.at[n])
        for n, (a, b) in enumerate(
            [(f_hbm, fin), (k_hbm, kin), (v_hbm, vin), (q_hbm, qin), (g_hbm, gin),
             (fwd_hbm, fwd), (fine_hbm, fine), (twist_hbm, twist), (bwd_hbm, bwd)]
        )
    ]
    for load in loads:
        load.start()
    before[...] = jnp.zeros(before.shape, BF16)
    after[...] = jnp.zeros(after.shape, F32)

    barrier = pltpu.get_barrier_semaphore()

    def greet_z(i, _):
        pl.semaphore_signal(barrier, inc=1, device_id=device(x, (z + i) % Z, yc), device_id_type=MESH)
        return 0

    def greet_w(i, _):
        there = (w + i) % W
        pl.semaphore_signal(barrier, inc=1, device_id=device(there // 8, z, there % 8), device_id_type=MESH)
        return 0

    lax.fori_loop(1, Z, greet_z, 0)
    lax.fori_loop(1, W, greet_w, 0)
    for neighbour in (next_device, last_device):
        pl.semaphore_signal(barrier, inc=1, device_id=neighbour, device_id_type=MESH)
    eye[...] = identity()

    def remote(src, dst, send, recv, to):
        return pltpu.make_async_remote_copy(
            src_ref=src, dst_ref=dst, send_sem=send, recv_sem=recv, device_id=to, device_id_type=MESH
        )

    def each(count, body, first=0):
        def step(i, _):
            body(i)
            return 0

        lax.fori_loop(first, count, step, 0)

    def columns_of(b):
        return pl.ds(pl.multiple_of(b * 256, 256), 256)

    def pack(p, code):
        def block(b):
            turned = lax.dot_general(
                eye[...], code(columns_of(b)).astype(BF16), (((1,), (1,)), ((), ())),
                preferred_element_type=F32,
            )
            snd[p, pl.ds(b * 2, 2)] = turned.reshape(2, W, 4, T).astype(BF16)

        each(Z // 2, block)

    def send_z(p, source):
        for n, dx in enumerate(ORDER):
            first = ((x + dx) % X) * 8
            target = mid.at[p, pl.ds(first, 8), z]

            def one(dz):
                zt = (z + dz) % Z
                remote(source(zt, first), target, zs_sem.at[p], zr_sem.at[p, n], device(x, zt, yc)).start()

            each(Z, one, 1)
            pltpu.make_async_copy(source(z, first), target, local_sem.at[p, n]).start()

    def target_of(p):
        if p < CONVOLVED:
            return rcv.at[p, x, :, yc]
        return back.at[p - CONVOLVED, :, w]

    def forward(p, n):
        dx = ORDER[n]
        xt = (x + dx) % X
        part = mid.at[p, pl.ds(xt * 8, 8), z]
        pltpu.make_async_copy(part, part, local_sem.at[p, n]).wait()
        arrived = mid.at[p, pl.ds(xt * 8, 8), pl.ds(0, Z - 1)]
        remote(arrived, arrived, zs_sem.at[p], zr_sem.at[p, n], here).wait_recv()
        target = target_of(p)

        def one(i):
            there = (yc + i) % 8
            remote(mid.at[p, xt * 8 + there], target, xs_sem.at[p], xr_sem.at[p], device(xt, z, there)).start()

        each(8, one, 1 if dx == 0 else 0)
        if dx == 0:
            pltpu.make_async_copy(mid.at[p, w], target, local_sem.at[p, X]).start()

    def await_all(p):
        pltpu.make_async_copy(mid.at[p, w], target_of(p), local_sem.at[p, X]).wait()
        part = mid.at[p, pl.ds(0, W - 1)]
        remote(part, part, xs_sem.at[p], xr_sem.at[p], here).wait_recv()

    def send_scale(n):
        def one(dz):
            remote(
                own_scale.at[n], mid_scale.at[n, z], scale_zs_sem.at[n], scale_zr_sem.at[n],
                device(x, (z + dz) % Z, yc),
            ).start()

        each(Z, one, 1)
        pltpu.make_async_copy(own_scale.at[n], mid_scale.at[n, z], scale_local_sem.at[n, 0]).start()

    def scale_target(n):
        if n == IN_SCALES:
            return in_scale.at[x, :, yc]
        return out_scale.at[n - 1, :, w]

    def forward_scale(n):
        pltpu.make_async_copy(own_scale.at[n], mid_scale.at[n, z], scale_local_sem.at[n, 0]).wait()
        arrived = mid_scale.at[n, pl.ds(0, Z - 1)]
        remote(arrived, arrived, scale_zs_sem.at[n], scale_zr_sem.at[n], here).wait_recv()

        def one(i):
            there = (w + i) % W
            remote(
                mid_scale.at[n], scale_target(n), scale_xs_sem.at[n], scale_xr_sem.at[n],
                device(there // 8, z, there % 8),
            ).start()

        each(W, one, 1)
        pltpu.make_async_copy(mid_scale.at[n], scale_target(n), scale_local_sem.at[n, 1]).start()

    def await_scale(n):
        pltpu.make_async_copy(mid_scale.at[n], scale_target(n), scale_local_sem.at[n, 1]).wait()
        part = out_scale.at[0, :, pl.ds(0, W - 1)]
        remote(part, part, scale_xs_sem.at[n], scale_xr_sem.at[n], here).wait_recv()

    def in_send(p):
        send_z(p, lambda zt, first: snd.at[p, zt, pl.ds(first, 8)])

    loads[0].wait()
    pack(FILTER, lambda cols: encode(fin[:, cols], FILTER_TOP))
    for load in loads[1:5]:
        load.wait()
    pl.semaphore_wait(barrier, Z + W)
    streams = (qin, kin, vin)
    halos = [
        remote(stream.at[pl.ds(T - 16, 16)], before.at[n], halo_s_sem.at[n], halo_r_sem.at[n], next_device)
        for n, stream in enumerate(streams)
    ]

    @pl.when(d != D - 1)
    def _():
        for halo in halos:
            halo.start()

    in_send(FILTER)

    @pl.when(d != 0)
    def _():
        for halo in halos:
            halo.wait_recv()

    tops[...] = jnp.zeros(tops.shape, F32)

    def gate_block(b):
        cols = columns_of(b)
        for n, stream in enumerate(streams):
            extended[n, 0:8, cols] = before[n, :, cols].astype(F32)[8:16]
            extended[n, 8 : T + 8, cols] = stream[:, cols].astype(F32)
            short[n, :, cols] = (
                taps[n, 0:1, cols] * extended[n, 8 : T + 8, cols]
                + taps[n, 1:2, cols] * extended[n, 7 : T + 7, cols]
                + taps[n, 2:3, cols] * extended[n, 6 : T + 6, cols]
            )
        value = short[1, :, cols] * short[2, :, cols]
        gated[:, cols] = value
        tops[0] = jnp.maximum(tops[0], jnp.max(jnp.abs(value).reshape(16, 8, 256), axis=0))
        value = gin[:, cols].astype(F32) * short[0, :, cols]
        grad_mixed[:, cols] = value
        tops[1] = jnp.maximum(tops[1], jnp.max(jnp.abs(value).reshape(16, 8, 256), axis=0))

    each(4, gate_block)

    def top_of(n):
        return jnp.maximum(jnp.max(tops[n], keepdims=True), 1e-30)

    gated_top, grad_top = top_of(0), top_of(1)
    first_half = lax.broadcasted_iota(jnp.int32, (1, T), 1) < T // 2
    own_scale[IN_SCALES] = jnp.where(first_half, gated_top, grad_top)
    pack(GATED, lambda cols: encode(gated[:, cols], gated_top))
    send_scale(IN_SCALES)
    in_send(GATED)
    pack(GRAD_MIXED, lambda cols: encode(grad_mixed[:, cols], grad_top))
    in_send(GRAD_MIXED)
    for load in loads[5:]:
        load.wait()

    def unpack(p):
        await_all(p)
        for b in range(X):
            rows[pl.ds(b * 256, 256)] = rcv[p, b].astype(F32).reshape(256, T)

    def row(j):
        return rows[pl.ds(j, D, stride=4), :]

    def put_columns(v, at):
        high, low = halves_of(v)
        work[0, 0:D, pl.ds(at * T, T)] = high
        work[1, 0:D, pl.ds(at * T, T)] = low

    def transform(out, pair):
        for b in range(2):
            part = pl.ds(b * D, D)
            high = work[0, 0:D]
            coarse[part] = (
                dot(fwd[0, part], high) + dot(fwd[1, part], high) + dot(fwd[0, part], work[1, 0:D])
            )
        tc, ts = twist[0], twist[1]
        for n in range(2):
            cols = pl.ds(n * T, T)
            re, im = coarse[0:D, cols], coarse[D : 2 * D, cols]
            both = jnp.concatenate([re * tc + im * ts, im * tc - re * ts], axis=1)
            high, low = halves_of(both)
            out[2 * pair + n] = (
                dot(high, fine[0, 0]) + dot(low, fine[0, 0]) + dot(high, fine[0, 1])
            )

    def untransform(left, right, conjugate, out, pair):
        tc, ts = twist[0], twist[1]
        for n in range(2):
            a, b = left[2 * pair + n], right[2 * pair + n]
            ar, ai, br, bi = a[:, 0:T], a[:, T:], b[:, 0:T], b[:, T:]
            if conjugate:
                re, im = ar * br + ai * bi, ar * bi - ai * br
            else:
                re, im = ar * br - ai * bi, ar * bi + ai * br
            high, low = halves_of(jnp.concatenate([re, im], axis=1))
            back_spec = dot(high, fine[1, 0]) + dot(low, fine[1, 0]) + dot(high, fine[1, 1])
            gr, gi = back_spec[:, 0:T], back_spec[:, T:]
            cols = pl.ds(n * T, T)
            high, low = halves_of(gr * tc - gi * ts)
            work[0, 0:D, cols] = high
            work[1, 0:D, cols] = low
            high, low = halves_of(gi * tc + gr * ts)
            work[0, D : 2 * D, cols] = high
            work[1, D : 2 * D, cols] = low
        value = dot(bwd[0], work[0]) + dot(bwd[1], work[0]) + dot(bwd[0], work[1])
        for n in range(2):
            out[2 * pair + n] = value[:, n * T : n * T + T]

    def filter_pair(pair):
        for n in range(2):
            put_columns(decode(row(2 * pair + n), FILTER_TOP), n)
        transform(spec.at[0], pair)

    def convolve_pair(half, conjugate):
        def body(pair):
            top = jnp.broadcast_to(
                in_scale[...].reshape(D, T)[:, half * 64 : half * 64 + 1], (D, T)
            )
            for n in range(2):
                put_columns(decode(row(2 * pair + n), top), n)
            transform(spec.at[1], pair)
            untransform(spec.at[0], spec.at[1], conjugate, result, pair)

        return body

    def out_send(p):
        top = jnp.max(jnp.max(jnp.abs(result[...]), axis=0), keepdims=True)
        top = jnp.maximum(top, 1e-30)
        own_scale[p - CONVOLVED + 1] = jnp.broadcast_to(top, (1, T))

        def code_row(j):
            rows[pl.ds(j, D, stride=4), :] = encode(result[j], top)

        each(4, code_row)
        for b in range(X):
            osnd[p - CONVOLVED, pl.ds(b * 8, 8)] = (
                rows[pl.ds(b * 256, 256)].reshape(Z, 8, 4, T).swapaxes(0, 1).astype(BF16)
            )
        send_scale(p - CONVOLVED + 1)
        send_z(p, lambda zt, first: osnd.at[p - CONVOLVED, pl.ds(first, 8), zt])

    for n in range(X):
        forward(FILTER, n)
    forward_scale(IN_SCALES)
    unpack(FILTER)
    each(2, filter_pair)
    for n in range(X):
        forward(GATED, n)
    await_scale(IN_SCALES)
    unpack(GATED)
    conv = convolve_pair(0, False)
    conv(0)
    for n in range(X):
        forward(GRAD_MIXED, n)
    conv(1)
    out_send(CONVOLVED)
    unpack(GRAD_MIXED)
    each(2, convolve_pair(1, True))
    out_send(GRAD_GATED)
    forward_scale(CONVOLVED_SCALE)
    for n in range(X):
        forward(CONVOLVED, n)
    forward_scale(GRAD_SCALE)

    def make_scale_row(n):
        await_scale(n + 1)
        owner = lax.broadcasted_iota(jnp.int32, (D, 1024), 0)
        channel = lax.broadcasted_iota(jnp.int32, (D, 1024), 1)
        top = jnp.tile(out_scale[n].reshape(D, T), (1, 8))
        scale_row[n : n + 1] = jnp.sum(jnp.where(channel // 4 == owner, top, 0.0), axis=0, keepdims=True)

    def returned(n, b):
        cols = columns_of(b)
        code = lax.dot_general(
            back[n, pl.ds(b * 2, 2)].reshape(256, T), eye[...], (((0,), (0,)), ((), ())),
            preferred_element_type=F32,
        )
        return decode(code, scale_row[n : n + 1, cols])

    def backward_halo(n):
        return remote(
            extended.at[n, pl.ds(0, 8)], after.at[n], halo_s_sem.at[3 + n], halo_r_sem.at[3 + n], last_device
        )

    def send_halo(n):
        @pl.when(d != 0)
        def _():
            backward_halo(n).start()

    def await_halo(n):
        @pl.when(d != D - 1)
        def _():
            backward_halo(n).wait_recv()

    def mix_block(b):
        cols = columns_of(b)
        mixed = returned(0, b) + skip[:, cols] * gated[:, cols]
        out_ref[:, cols] = (short[0, :, cols] * mixed).astype(BF16)
        extended[0, 0:T, cols] = gin[:, cols].astype(F32) * mixed

    def grad_block(b):
        cols = columns_of(b)
        total = returned(1, b) + skip[:, cols] * grad_mixed[:, cols]
        extended[1, 0:T, cols] = total * short[2, :, cols]
        extended[2, 0:T, cols] = total * short[1, :, cols]

    def finish(n, ref):
        def block(b):
            cols = columns_of(b)
            extended[n, T : T + 8, cols] = after[n, :, cols]
            ref[:, cols] = (
                taps[n, 0:1, cols] * extended[n, 0:T, cols]
                + taps[n, 1:2, cols] * extended[n, 1 : T + 1, cols]
                + taps[n, 2:3, cols] * extended[n, 2 : T + 2, cols]
            ).astype(BF16)

        each(4, block)

    make_scale_row(0)
    await_all(CONVOLVED)
    each(4, mix_block)
    send_halo(0)
    for n in range(X):
        forward(GRAD_GATED, n)
    make_scale_row(1)
    await_all(GRAD_GATED)
    each(4, grad_block)
    send_halo(1)
    send_halo(2)
    await_halo(0)
    finish(0, grad_q_ref)
    await_halo(1)
    finish(1, grad_k_ref)
    await_halo(2)
    finish(2, grad_v_ref)

    @pl.when(d != D - 1)
    def _():
        for halo in halos:
            halo.wait_send()

    @pl.when(d != 0)
    def _():
        for n in range(3):
            backward_halo(n).wait_send()

    for p in range(5):
        sent = mid.at[p, pl.ds(0, W - 1)]
        remote(sent, sent, xs_sem.at[p], xr_sem.at[p], here).wait_send()
        sent = mid.at[p, :, pl.ds(0, Z - 1)]
        remote(sent, sent, zs_sem.at[p], zr_sem.at[p, 0], here).wait_send()
    for n in range(3):
        sent = out_scale.at[0, :, pl.ds(0, W - 1)]
        remote(sent, sent, scale_xs_sem.at[n], scale_xr_sem.at[n], here).wait_send()
        sent = mid_scale.at[n, pl.ds(0, Z - 1)]
        remote(sent, sent, scale_zs_sem.at[n], scale_zr_sem.at[n], here).wait_send()


def local(query_in, key_in, value_in, conv_taps, long_filter, skip_gain, grad_out):
    forward, backward, fine, twist = (jnp.asarray(m) for m in dft_constants())
    anywhere = pl.BlockSpec(memory_space=pltpu.HBM)
    vmem = pl.BlockSpec(memory_space=pltpu.VMEM)
    tokens = pltpu.VMEM((T, 1024), BF16)
    wide = pltpu.VMEM((T, 1024), F32)
    result = jax.ShapeDtypeStruct((T, 1024), BF16)
    dma = pltpu.SemaphoreType.DMA
    return tuple(
        pl.pallas_call(
            main_kernel,
            out_shape=(result,) * 4,
            in_specs=[anywhere] * 5 + [vmem] * 2 + [anywhere] * 4,
            out_specs=(vmem,) * 4,
            scratch_shapes=[
                tokens, tokens, tokens, tokens, wide,
                pltpu.VMEM(forward.shape, BF16),
                pltpu.VMEM(backward.shape, BF16),
                pltpu.VMEM(fine.shape, BF16),
                pltpu.VMEM(twist.shape, F32),
                pltpu.VMEM((256, 256), BF16),
                pltpu.VMEM((3, Z, W, 4, T), BF16),
                pltpu.VMEM((5, W, Z, 4, T), BF16),
                pltpu.VMEM((3, X, Z, 8, 4, T), BF16),
                pltpu.VMEM((4 * D, T), F32),
                pltpu.VMEM((2, 4, D, 2 * T), F32),
                pltpu.VMEM((2 * D, 2 * T), F32),
                pltpu.VMEM((2, 2 * D, 2 * T), BF16),
                pltpu.VMEM((4, D, T), F32),
                pltpu.VMEM((3, T + 8, 1024), F32),
                pltpu.VMEM((3, T, 1024), F32),
                wide, wide,
                pltpu.VMEM((2, 8, 256), F32),
                pltpu.VMEM((2, W, Z, 4, T), BF16),
                pltpu.VMEM((2, Z, W, 4, T), BF16),
                pltpu.VMEM((3, 16, 1024), BF16),
                pltpu.VMEM((3, 8, 1024), F32),
                pltpu.VMEM((3, 1, T), F32),
                pltpu.VMEM((3, Z, 1, T), F32),
                pltpu.VMEM((X, Z, 8, 1, T), F32),
                pltpu.VMEM((2, Z, W, 1, T), F32),
                pltpu.VMEM((2, 1024), F32),
                dma((9,)), dma((5, X + 1)), dma((5,)), dma((5, X)), dma((5,)), dma((5,)),
                dma((6,)), dma((6,)),
                dma((3, 2)), dma((3,)), dma((3,)), dma((3,)), dma((3,)),
            ],
            compiler_params=pltpu.CompilerParams(
                collective_id=0, has_side_effects=True, vmem_limit_bytes=67043328
            ),
            name="hyena_exchange",
        )(
            query_in, key_in, value_in, grad_out, long_filter, conv_taps, skip_gain.reshape(1, 1024),
            forward, backward, fine, twist,
        )
    )


def solution(mesh):
    tokens = P(("outer", "inner"), None)
    return jax.shard_map(
        local,
        mesh=mesh,
        in_specs=(tokens, tokens, tokens, P(), tokens, P(), tokens),
        out_specs=(tokens,) * 4,
        check_vma=False,
    )
```

```python
import functools

import jax
import jax.numpy as jnp
import numpy as np
from jax import lax
from jax.experimental import pallas as pl
from jax.experimental.pallas import tpu as pltpu
from jax.sharding import PartitionSpec as P

MESH = pl.DeviceIdType.MESH
F32, BF16 = jnp.float32, jnp.bfloat16
X, Z, Y, C = 4, 8, 4, 2
W = X * Y * C
D = 256
T = 128
POINTS = 2 * D * T


def dft_constants():
    k = np.arange(D)[:, None] + 0.5
    d = np.arange(D)[None, :]
    coarse = 2 * np.pi * (k * d / (2 * D) % 1.0)
    forward = np.concatenate([np.cos(coarse), -np.sin(coarse)], 0)
    backward = np.concatenate([np.cos(coarse).T, -np.sin(coarse).T], 1) * (2.0 / POINTS)
    t = np.arange(T)[None, :]
    turn = 2 * np.pi * (k * t / POINTS % 1.0)
    fine = 2 * np.pi * (t.T * t % T) / T
    c, s = np.cos(fine), np.sin(fine)
    fine_forward = np.block([[c, -s], [s, c]])
    fine_backward = np.block([[c, s], [-s, c]])

    def halves(m):
        m = m.astype(np.float32)
        high = m.astype(jnp.bfloat16)
        low = (m - high.astype(np.float32)).astype(jnp.bfloat16)
        return np.stack([high, low])

    fine_both = np.stack([halves(fine_forward), halves(fine_backward)])
    twist = np.stack([np.cos(turn), np.sin(turn)]).astype(np.float32)
    return halves(forward), halves(backward), fine_both, twist


def place():
    o, i = lax.axis_index("outer"), lax.axis_index("inner")
    return o // 4, (o % 4) * 2 + i // 8, i % 8


def device(x, z, yc):
    return (x * 4 + z // 2, (z % 2) * 8 + yc)


def halves_of(v):
    high = v.astype(BF16)
    return high, (v - high.astype(F32)).astype(BF16)


def dot(a, b):
    return jnp.dot(a, b, preferred_element_type=F32)


def identity():
    r = lax.broadcasted_iota(jnp.int32, (256, 256), 0)
    c = lax.broadcasted_iota(jnp.int32, (256, 256), 1)
    return jnp.where(r == c, 1.0, 0.0).astype(BF16)


FILTER, GATED, GRAD_MIXED, CONVOLVED, GRAD_GATED = range(5)
ORDER = (2, 1, 3, 0)
IN_SCALES, CONVOLVED_SCALE, GRAD_SCALE = range(3)

RATIO = 256.0
SHIFT = 124.0 * float(np.log(2.0))
SLOPE = 2.0 * SHIFT / float(np.log(1.0 + RATIO))
FILTER_TOP = 1.125


def encode(v, top):
    size = jnp.exp(SLOPE * jnp.log(1.0 + jnp.abs(v) * (RATIO / top)) - SHIFT)
    return jnp.where(v < 0.0, -size, size)


def decode(code, top):
    size = (jnp.exp((jnp.log(jnp.abs(code)) + SHIFT) * (1.0 / SLOPE)) - 1.0) * (top / RATIO)
    return jnp.where(code < 0.0, -size, size)


def main_kernel(
    q_hbm, k_hbm, v_hbm, g_hbm, f_hbm, taps, skip, fwd_hbm, bwd_hbm, fine_hbm, twist_hbm,
    out_ref, grad_q_ref, grad_k_ref, grad_v_ref,
    kin, vin, qin, gin, fin, fwd, bwd, fine, twist,
    eye, snd, mid, rcv, rows, spec, coarse, work, result, extended, short, gated, grad_mixed, tops,
    osnd, back, before, after, own_scale, mid_scale, in_scale, out_scale, scale_row,
    in_sem, local_sem, zs_sem, zr_sem, xs_sem, xr_sem, halo_s_sem, halo_r_sem,
    scale_local_sem, scale_zs_sem, scale_zr_sem, scale_xs_sem, scale_xr_sem,
):
    x, z, yc = place()
    w = x * 8 + yc
    d = x * 64 + z * 8 + yc
    next_d, last_d = (d + 1) % D, (d + D - 1) % D
    next_device = device(next_d // 64, (next_d // 8) % 8, next_d % 8)
    last_device = device(last_d // 64, (last_d // 8) % 8, last_d % 8)
    here = device(x, z, yc)

    loads = [
        pltpu.make_async_copy(a, b, in_sem.at[n])
        for n, (a, b) in enumerate(
            [(f_hbm, fin), (k_hbm, kin), (v_hbm, vin), (q_hbm, qin), (g_hbm, gin),
             (fwd_hbm, fwd), (fine_hbm, fine), (twist_hbm, twist), (bwd_hbm, bwd)]
        )
    ]
    for load in loads:
        load.start()
    before[...] = jnp.zeros(before.shape, BF16)
    after[...] = jnp.zeros(after.shape, F32)

    barrier = pltpu.get_barrier_semaphore()

    def greet_z(i, _):
        pl.semaphore_signal(barrier, inc=1, device_id=device(x, (z + i) % Z, yc), device_id_type=MESH)
        return 0

    def greet_w(i, _):
        there = (w + i) % W
        pl.semaphore_signal(barrier, inc=1, device_id=device(there // 8, z, there % 8), device_id_type=MESH)
        return 0

    lax.fori_loop(1, Z, greet_z, 0)
    lax.fori_loop(1, W, greet_w, 0)
    for neighbour in (next_device, last_device):
        pl.semaphore_signal(barrier, inc=1, device_id=neighbour, device_id_type=MESH)
    eye[...] = identity()

    def remote(src, dst, send, recv, to):
        return pltpu.make_async_remote_copy(
            src_ref=src, dst_ref=dst, send_sem=send, recv_sem=recv, device_id=to, device_id_type=MESH
        )

    def each(count, body, first=0):
        def step(i, _):
            body(i)
            return 0

        lax.fori_loop(first, count, step, 0)

    def all_of(count, body, first=0):
        for i in range(first, count):
            body(i)

    def columns_of(b):
        return pl.ds(pl.multiple_of(b * 256, 256), 256)

    def pack(p, code):
        def block(b):
            turned = lax.dot_general(
                eye[...], code(columns_of(b)).astype(BF16), (((1,), (1,)), ((), ())),
                preferred_element_type=F32,
            )
            snd[p, pl.ds(b * 2, 2)] = turned.reshape(2, W, 4, T).astype(BF16)

        each(Z // 2, block)

    def send_z(p, source):
        for n, dx in enumerate(ORDER):
            first = ((x + dx) % X) * 8
            target = mid.at[p, pl.ds(first, 8), z]

            def one(dz):
                zt = (z + dz) % Z
                remote(source(zt, first), target, zs_sem.at[p], zr_sem.at[p, n], device(x, zt, yc)).start()

            all_of(Z, one, 1)
            pltpu.make_async_copy(source(z, first), target, local_sem.at[p, n]).start()

    def target_of(p):
        if p < CONVOLVED:
            return rcv.at[p, x, :, yc]
        return back.at[p - CONVOLVED, :, w]

    def forward(p, n):
        dx = ORDER[n]
        xt = (x + dx) % X
        part = mid.at[p, pl.ds(xt * 8, 8), z]
        pltpu.make_async_copy(part, part, local_sem.at[p, n]).wait()
        arrived = mid.at[p, pl.ds(xt * 8, 8), pl.ds(0, Z - 1)]
        remote(arrived, arrived, zs_sem.at[p], zr_sem.at[p, n], here).wait_recv()
        target = target_of(p)

        def one(i):
            there = (yc + i) % 8
            remote(mid.at[p, xt * 8 + there], target, xs_sem.at[p], xr_sem.at[p], device(xt, z, there)).start()

        all_of(8, one, 1 if dx == 0 else 0)
        if dx == 0:
            pltpu.make_async_copy(mid.at[p, w], target, local_sem.at[p, X]).start()

    def await_all(p):
        pltpu.make_async_copy(mid.at[p, w], target_of(p), local_sem.at[p, X]).wait()
        part = mid.at[p, pl.ds(0, W - 1)]
        remote(part, part, xs_sem.at[p], xr_sem.at[p], here).wait_recv()

    def send_scale(n):
        def one(dz):
            remote(
                own_scale.at[n], mid_scale.at[n, z], scale_zs_sem.at[n], scale_zr_sem.at[n],
                device(x, (z + dz) % Z, yc),
            ).start()

        all_of(Z, one, 1)
        pltpu.make_async_copy(own_scale.at[n], mid_scale.at[n, z], scale_local_sem.at[n, 0]).start()

    def scale_target(n):
        if n == IN_SCALES:
            return in_scale.at[x, :, yc]
        return out_scale.at[n - 1, :, w]

    def forward_scale(n):
        pltpu.make_async_copy(own_scale.at[n], mid_scale.at[n, z], scale_local_sem.at[n, 0]).wait()
        arrived = mid_scale.at[n, pl.ds(0, Z - 1)]
        remote(arrived, arrived, scale_zs_sem.at[n], scale_zr_sem.at[n], here).wait_recv()

        def one(i):
            there = (w + i) % W
            remote(
                mid_scale.at[n], scale_target(n), scale_xs_sem.at[n], scale_xr_sem.at[n],
                device(there // 8, z, there % 8),
            ).start()

        all_of(W, one, 1)
        pltpu.make_async_copy(mid_scale.at[n], scale_target(n), scale_local_sem.at[n, 1]).start()

    def await_scale(n):
        pltpu.make_async_copy(mid_scale.at[n], scale_target(n), scale_local_sem.at[n, 1]).wait()
        part = out_scale.at[0, :, pl.ds(0, W - 1)]
        remote(part, part, scale_xs_sem.at[n], scale_xr_sem.at[n], here).wait_recv()

    def in_send(p):
        send_z(p, lambda zt, first: snd.at[p, zt, pl.ds(first, 8)])

    loads[0].wait()
    pack(FILTER, lambda cols: encode(fin[:, cols], FILTER_TOP))
    for load in loads[1:5]:
        load.wait()
    pl.semaphore_wait(barrier, Z + W)
    streams = (qin, kin, vin)
    halos = [
        remote(stream.at[pl.ds(T - 16, 16)], before.at[n], halo_s_sem.at[n], halo_r_sem.at[n], next_device)
        for n, stream in enumerate(streams)
    ]

    @pl.when(d != D - 1)
    def _():
        for halo in halos:
            halo.start()

    in_send(FILTER)

    @pl.when(d != 0)
    def _():
        for halo in halos:
            halo.wait_recv()

    tops[...] = jnp.zeros(tops.shape, F32)

    def gate_block(b):
        cols = columns_of(b)
        for n, stream in enumerate(streams):
            extended[n, 0:8, cols] = before[n, :, cols].astype(F32)[8:16]
            extended[n, 8 : T + 8, cols] = stream[:, cols].astype(F32)
            short[n, :, cols] = (
                taps[n, 0:1, cols] * extended[n, 8 : T + 8, cols]
                + taps[n, 1:2, cols] * extended[n, 7 : T + 7, cols]
                + taps[n, 2:3, cols] * extended[n, 6 : T + 6, cols]
            )
        value = short[1, :, cols] * short[2, :, cols]
        gated[:, cols] = value
        tops[0] = jnp.maximum(tops[0], jnp.max(jnp.abs(value).reshape(16, 8, 256), axis=0))
        value = gin[:, cols].astype(F32) * short[0, :, cols]
        grad_mixed[:, cols] = value
        tops[1] = jnp.maximum(tops[1], jnp.max(jnp.abs(value).reshape(16, 8, 256), axis=0))

    each(4, gate_block)

    def top_of(n):
        return jnp.maximum(jnp.max(tops[n], keepdims=True), 1e-30)

    gated_top, grad_top = top_of(0), top_of(1)
    first_half = lax.broadcasted_iota(jnp.int32, (1, T), 1) < T // 2
    own_scale[IN_SCALES] = jnp.where(first_half, gated_top, grad_top)
    pack(GATED, lambda cols: encode(gated[:, cols], gated_top))
    send_scale(IN_SCALES)
    in_send(GATED)
    pack(GRAD_MIXED, lambda cols: encode(grad_mixed[:, cols], grad_top))
    in_send(GRAD_MIXED)
    for load in loads[5:]:
        load.wait()

    def unpack(p):
        await_all(p)
        for b in range(X):
            rows[pl.ds(b * 256, 256)] = rcv[p, b].astype(F32).reshape(256, T)

    def row(j):
        return rows[pl.ds(j, D, stride=4), :]

    def put_columns(v, at):
        high, low = halves_of(v)
        work[0, 0:D, pl.ds(at * T, T)] = high
        work[1, 0:D, pl.ds(at * T, T)] = low

    def transform(out, pair):
        for b in range(2):
            part = pl.ds(b * D, D)
            high = work[0, 0:D]
            coarse[part] = (
                dot(fwd[0, part], high) + dot(fwd[1, part], high) + dot(fwd[0, part], work[1, 0:D])
            )
        tc, ts = twist[0], twist[1]
        for n in range(2):
            cols = pl.ds(n * T, T)
            re, im = coarse[0:D, cols], coarse[D : 2 * D, cols]
            both = jnp.concatenate([re * tc + im * ts, im * tc - re * ts], axis=1)
            high, low = halves_of(both)
            out[2 * pair + n] = (
                dot(high, fine[0, 0]) + dot(low, fine[0, 0]) + dot(high, fine[0, 1])
            )

    def untransform(left, right, conjugate, out, pair):
        tc, ts = twist[0], twist[1]
        for n in range(2):
            a, b = left[2 * pair + n], right[2 * pair + n]
            ar, ai, br, bi = a[:, 0:T], a[:, T:], b[:, 0:T], b[:, T:]
            if conjugate:
                re, im = ar * br + ai * bi, ar * bi - ai * br
            else:
                re, im = ar * br - ai * bi, ar * bi + ai * br
            high, low = halves_of(jnp.concatenate([re, im], axis=1))
            back_spec = dot(high, fine[1, 0]) + dot(low, fine[1, 0]) + dot(high, fine[1, 1])
            gr, gi = back_spec[:, 0:T], back_spec[:, T:]
            cols = pl.ds(n * T, T)
            high, low = halves_of(gr * tc - gi * ts)
            work[0, 0:D, cols] = high
            work[1, 0:D, cols] = low
            high, low = halves_of(gi * tc + gr * ts)
            work[0, D : 2 * D, cols] = high
            work[1, D : 2 * D, cols] = low
        value = dot(bwd[0], work[0]) + dot(bwd[1], work[0]) + dot(bwd[0], work[1])
        for n in range(2):
            out[2 * pair + n] = value[:, n * T : n * T + T]

    def filter_pair(pair):
        for n in range(2):
            put_columns(decode(row(2 * pair + n), FILTER_TOP), n)
        transform(spec.at[0], pair)

    def convolve_pair(half, conjugate):
        def body(pair):
            top = jnp.broadcast_to(
                in_scale[...].reshape(D, T)[:, half * 64 : half * 64 + 1], (D, T)
            )
            for n in range(2):
                put_columns(decode(row(2 * pair + n), top), n)
            transform(spec.at[1], pair)
            untransform(spec.at[0], spec.at[1], conjugate, result, pair)

        return body

    def out_send(p):
        top = jnp.max(jnp.max(jnp.abs(result[...]), axis=0), keepdims=True)
        top = jnp.maximum(top, 1e-30)
        own_scale[p - CONVOLVED + 1] = jnp.broadcast_to(top, (1, T))

        def code_row(j):
            rows[pl.ds(j, D, stride=4), :] = encode(result[j], top)

        each(4, code_row)
        for b in range(X):
            osnd[p - CONVOLVED, pl.ds(b * 8, 8)] = (
                rows[pl.ds(b * 256, 256)].reshape(Z, 8, 4, T).swapaxes(0, 1).astype(BF16)
            )
        send_scale(p - CONVOLVED + 1)
        send_z(p, lambda zt, first: osnd.at[p - CONVOLVED, pl.ds(first, 8), zt])

    for n in range(X):
        forward(FILTER, n)
    forward_scale(IN_SCALES)
    unpack(FILTER)
    each(2, filter_pair)
    for n in range(X):
        forward(GATED, n)
    await_scale(IN_SCALES)
    unpack(GATED)
    conv = convolve_pair(0, False)
    conv(0)
    for n in range(X):
        forward(GRAD_MIXED, n)
    conv(1)
    out_send(CONVOLVED)
    unpack(GRAD_MIXED)
    each(2, convolve_pair(1, True))
    out_send(GRAD_GATED)
    forward_scale(CONVOLVED_SCALE)
    for n in range(X):
        forward(CONVOLVED, n)
    forward_scale(GRAD_SCALE)

    def make_scale_row(n):
        await_scale(n + 1)
        owner = lax.broadcasted_iota(jnp.int32, (D, 1024), 0)
        channel = lax.broadcasted_iota(jnp.int32, (D, 1024), 1)
        top = jnp.tile(out_scale[n].reshape(D, T), (1, 8))
        scale_row[n : n + 1] = jnp.sum(jnp.where(channel // 4 == owner, top, 0.0), axis=0, keepdims=True)

    def returned(n, b):
        cols = columns_of(b)
        code = lax.dot_general(
            back[n, pl.ds(b * 2, 2)].reshape(256, T), eye[...], (((0,), (0,)), ((), ())),
            preferred_element_type=F32,
        )
        return decode(code, scale_row[n : n + 1, cols])

    def backward_halo(n):
        return remote(
            extended.at[n, pl.ds(0, 8)], after.at[n], halo_s_sem.at[3 + n], halo_r_sem.at[3 + n], last_device
        )

    def send_halo(n):
        @pl.when(d != 0)
        def _():
            backward_halo(n).start()

    def await_halo(n):
        @pl.when(d != D - 1)
        def _():
            backward_halo(n).wait_recv()

    def mix_block(b):
        cols = columns_of(b)
        mixed = returned(0, b) + skip[:, cols] * gated[:, cols]
        out_ref[:, cols] = (short[0, :, cols] * mixed).astype(BF16)
        extended[0, 0:T, cols] = gin[:, cols].astype(F32) * mixed

    def grad_block(b):
        cols = columns_of(b)
        total = returned(1, b) + skip[:, cols] * grad_mixed[:, cols]
        extended[1, 0:T, cols] = total * short[2, :, cols]
        extended[2, 0:T, cols] = total * short[1, :, cols]

    def finish(n, ref):
        def block(b):
            cols = columns_of(b)
            extended[n, T : T + 8, cols] = after[n, :, cols]
            ref[:, cols] = (
                taps[n, 0:1, cols] * extended[n, 0:T, cols]
                + taps[n, 1:2, cols] * extended[n, 1 : T + 1, cols]
                + taps[n, 2:3, cols] * extended[n, 2 : T + 2, cols]
            ).astype(BF16)

        each(4, block)

    make_scale_row(0)
    await_all(CONVOLVED)
    each(4, mix_block)
    send_halo(0)
    for n in range(X):
        forward(GRAD_GATED, n)
    make_scale_row(1)
    await_all(GRAD_GATED)
    each(4, grad_block)
    send_halo(1)
    send_halo(2)
    await_halo(0)
    finish(0, grad_q_ref)
    await_halo(1)
    finish(1, grad_k_ref)
    await_halo(2)
    finish(2, grad_v_ref)

    @pl.when(d != D - 1)
    def _():
        for halo in halos:
            halo.wait_send()

    @pl.when(d != 0)
    def _():
        for n in range(3):
            backward_halo(n).wait_send()

    for p in range(5):
        sent = mid.at[p, pl.ds(0, W - 1)]
        remote(sent, sent, xs_sem.at[p], xr_sem.at[p], here).wait_send()
        sent = mid.at[p, :, pl.ds(0, Z - 1)]
        remote(sent, sent, zs_sem.at[p], zr_sem.at[p, 0], here).wait_send()
    for n in range(3):
        sent = out_scale.at[0, :, pl.ds(0, W - 1)]
        remote(sent, sent, scale_xs_sem.at[n], scale_xr_sem.at[n], here).wait_send()
        sent = mid_scale.at[n, pl.ds(0, Z - 1)]
        remote(sent, sent, scale_zs_sem.at[n], scale_zr_sem.at[n], here).wait_send()


def hand_on_kernel(*refs):
    ins, outs, (held, in_sem, out_sem) = refs[:4], refs[4:8], refs[8:]
    inward = [pltpu.make_async_copy(ins[n], held.at[n], in_sem.at[n]) for n in range(4)]
    outward = [pltpu.make_async_copy(held.at[n], outs[n], out_sem.at[n]) for n in range(4)]
    for copy in inward:
        copy.start()
    for n in range(4):
        inward[n].wait()
        outward[n].start()
    for copy in outward:
        copy.wait()


def local(query_in, key_in, value_in, conv_taps, long_filter, skip_gain, grad_out):
    forward, backward, fine, twist = (jnp.asarray(m) for m in dft_constants())
    anywhere = pl.BlockSpec(memory_space=pltpu.HBM)
    vmem = pl.BlockSpec(memory_space=pltpu.VMEM)
    tokens = pltpu.VMEM((T, 1024), BF16)
    wide = pltpu.VMEM((T, 1024), F32)
    result = jax.ShapeDtypeStruct((T, 1024), BF16)
    dma = pltpu.SemaphoreType.DMA
    outs = pl.pallas_call(
        main_kernel,
        out_shape=(result,) * 4,
        in_specs=[anywhere] * 5 + [vmem] * 2 + [anywhere] * 4,
        out_specs=(vmem,) * 4,
        scratch_shapes=[
            tokens, tokens, tokens, tokens, wide,
            pltpu.VMEM(forward.shape, BF16),
            pltpu.VMEM(backward.shape, BF16),
            pltpu.VMEM(fine.shape, BF16),
            pltpu.VMEM(twist.shape, F32),
            pltpu.VMEM((256, 256), BF16),
            pltpu.VMEM((3, Z, W, 4, T), BF16),
            pltpu.VMEM((5, W, Z, 4, T), BF16),
            pltpu.VMEM((3, X, Z, 8, 4, T), BF16),
            pltpu.VMEM((4 * D, T), F32),
            pltpu.VMEM((2, 4, D, 2 * T), F32),
            pltpu.VMEM((2 * D, 2 * T), F32),
            pltpu.VMEM((2, 2 * D, 2 * T), BF16),
            pltpu.VMEM((4, D, T), F32),
            pltpu.VMEM((3, T + 8, 1024), F32),
            pltpu.VMEM((3, T, 1024), F32),
            wide, wide,
            pltpu.VMEM((2, 8, 256), F32),
            pltpu.VMEM((2, W, Z, 4, T), BF16),
            pltpu.VMEM((2, Z, W, 4, T), BF16),
            pltpu.VMEM((3, 16, 1024), BF16),
            pltpu.VMEM((3, 8, 1024), F32),
            pltpu.VMEM((3, 1, T), F32),
            pltpu.VMEM((3, Z, 1, T), F32),
            pltpu.VMEM((X, Z, 8, 1, T), F32),
            pltpu.VMEM((2, Z, W, 1, T), F32),
            pltpu.VMEM((2, 1024), F32),
            dma((9,)), dma((5, X + 1)), dma((5,)), dma((5, X)), dma((5,)), dma((5,)),
            dma((6,)), dma((6,)),
            dma((3, 2)), dma((3,)), dma((3,)), dma((3,)), dma((3,)),
        ],
        compiler_params=pltpu.CompilerParams(
            collective_id=0, has_side_effects=True, vmem_limit_bytes=67043328
        ),
        name="hyena_exchange",
    )(
        query_in, key_in, value_in, grad_out, long_filter, conv_taps, skip_gain.reshape(1, 1024),
        forward, backward, fine, twist,
    )
    anyhow = pl.BlockSpec(memory_space=pltpu.HBM)
    return tuple(
        pl.pallas_call(
            hand_on_kernel,
            out_shape=(result,) * 4,
            in_specs=[anyhow] * 4,
            out_specs=(anyhow,) * 4,
            scratch_shapes=[pltpu.VMEM((4, T, 1024), BF16), dma((4,)), dma((4,))],
            compiler_params=pltpu.CompilerParams(vmem_limit_bytes=67043328),
            name="hyena_hand_on",
        )(*outs)
    )


def solution(mesh):
    tokens = P(("outer", "inner"), None)
    return jax.shard_map(
        local,
        mesh=mesh,
        in_specs=(tokens, tokens, tokens, P(), tokens, P(), tokens),
        out_specs=(tokens,) * 4,
        check_vma=False,
    )
```

```python
import functools

import jax
import jax.numpy as jnp
import numpy as np
from jax import lax
from jax.experimental import pallas as pl
from jax.experimental.pallas import tpu as pltpu
from jax.sharding import PartitionSpec as P

MESH = pl.DeviceIdType.MESH
F32, BF16 = jnp.float32, jnp.bfloat16
X, Z, Y, C = 4, 8, 4, 2
W = X * Y * C
D = 256
T = 128
POINTS = 2 * D * T


def dft_constants():
    k = np.arange(D)[:, None] + 0.5
    d = np.arange(D)[None, :]
    coarse = 2 * np.pi * (k * d / (2 * D) % 1.0)
    forward = np.concatenate([np.cos(coarse), -np.sin(coarse)], 0)
    backward = np.concatenate([np.cos(coarse).T, -np.sin(coarse).T], 1) * (2.0 / POINTS)
    t = np.arange(T)[None, :]
    turn = 2 * np.pi * (k * t / POINTS % 1.0)
    fine = 2 * np.pi * (t.T * t % T) / T
    c, s = np.cos(fine), np.sin(fine)
    fine_forward = np.block([[c, -s], [s, c]])
    fine_backward = np.block([[c, s], [-s, c]])

    def halves(m):
        m = m.astype(np.float32)
        high = m.astype(jnp.bfloat16)
        low = (m - high.astype(np.float32)).astype(jnp.bfloat16)
        return np.stack([high, low])

    fine_both = np.stack([halves(fine_forward), halves(fine_backward)])
    twist = np.stack([np.cos(turn), np.sin(turn)]).astype(np.float32)
    return halves(forward), halves(backward), fine_both, twist


def place():
    o, i = lax.axis_index("outer"), lax.axis_index("inner")
    return o // 4, (o % 4) * 2 + i // 8, i % 8


def device(x, z, yc):
    return (x * 4 + z // 2, (z % 2) * 8 + yc)


def halves_of(v):
    high = v.astype(BF16)
    return high, (v - high.astype(F32)).astype(BF16)


def dot(a, b):
    return jnp.dot(a, b, preferred_element_type=F32)


def identity():
    r = lax.broadcasted_iota(jnp.int32, (256, 256), 0)
    c = lax.broadcasted_iota(jnp.int32, (256, 256), 1)
    return jnp.where(r == c, 1.0, 0.0).astype(BF16)


FILTER, GATED, GRAD_MIXED, CONVOLVED, GRAD_GATED = range(5)
ORDER = (2, 1, 3, 0)
IN_SCALES, CONVOLVED_SCALE, GRAD_SCALE = range(3)

RATIO = 256.0
SHIFT = 124.0 * float(np.log(2.0))
SLOPE = 2.0 * SHIFT / float(np.log(1.0 + RATIO))
FILTER_TOP = 1.125


def encode(v, top):
    size = jnp.exp(SLOPE * jnp.log(1.0 + jnp.abs(v) * (RATIO / top)) - SHIFT)
    return jnp.where(v < 0.0, -size, size)


def decode(code, top):
    size = (jnp.exp((jnp.log(jnp.abs(code)) + SHIFT) * (1.0 / SLOPE)) - 1.0) * (top / RATIO)
    return jnp.where(code < 0.0, -size, size)


def main_kernel(
    q_hbm, k_hbm, v_hbm, g_hbm, f_hbm, taps, skip, fwd_hbm, bwd_hbm, fine_hbm, twist_hbm,
    out_hbm, grad_q_hbm, grad_k_hbm, grad_v_hbm,
    kin, vin, qin, gin, fin, fwd, bwd, fine, twist,
    eye, snd, mid, rcv, rows, spec, coarse, work, result, extended, short, gated, grad_mixed, tops,
    osnd, back, before, after, own_scale, mid_scale, in_scale, out_scale, scale_row, held,
    in_sem, held_sem, local_sem, zs_sem, zr_sem, xs_sem, xr_sem, halo_s_sem, halo_r_sem,
    scale_local_sem, scale_zs_sem, scale_zr_sem, scale_xs_sem, scale_xr_sem,
):
    x, z, yc = place()
    w = x * 8 + yc
    d = x * 64 + z * 8 + yc
    next_d, last_d = (d + 1) % D, (d + D - 1) % D
    next_device = device(next_d // 64, (next_d // 8) % 8, next_d % 8)
    last_device = device(last_d // 64, (last_d // 8) % 8, last_d % 8)
    here = device(x, z, yc)

    loads = [
        pltpu.make_async_copy(a, b, in_sem.at[n])
        for n, (a, b) in enumerate(
            [(f_hbm, fin), (k_hbm, kin), (v_hbm, vin), (q_hbm, qin), (g_hbm, gin),
             (fwd_hbm, fwd), (fine_hbm, fine), (twist_hbm, twist), (bwd_hbm, bwd)]
        )
    ]
    for load in loads:
        load.start()
    before[...] = jnp.zeros(before.shape, BF16)
    after[...] = jnp.zeros(after.shape, F32)

    barrier = pltpu.get_barrier_semaphore()

    def greet_z(i, _):
        pl.semaphore_signal(barrier, inc=1, device_id=device(x, (z + i) % Z, yc), device_id_type=MESH)
        return 0

    def greet_w(i, _):
        there = (w + i) % W
        pl.semaphore_signal(barrier, inc=1, device_id=device(there // 8, z, there % 8), device_id_type=MESH)
        return 0

    lax.fori_loop(1, Z, greet_z, 0)
    lax.fori_loop(1, W, greet_w, 0)
    for neighbour in (next_device, last_device):
        pl.semaphore_signal(barrier, inc=1, device_id=neighbour, device_id_type=MESH)
    eye[...] = identity()

    def remote(src, dst, send, recv, to):
        return pltpu.make_async_remote_copy(
            src_ref=src, dst_ref=dst, send_sem=send, recv_sem=recv, device_id=to, device_id_type=MESH
        )

    def each(count, body, first=0):
        def step(i, _):
            body(i)
            return 0

        lax.fori_loop(first, count, step, 0)

    def all_of(count, body, first=0):
        for i in range(first, count):
            body(i)

    def columns_of(b):
        return pl.ds(pl.multiple_of(b * 256, 256), 256)

    def pack(p, code):
        def block(b):
            turned = lax.dot_general(
                eye[...], code(columns_of(b)).astype(BF16), (((1,), (1,)), ((), ())),
                preferred_element_type=F32,
            )
            snd[p, pl.ds(b * 2, 2)] = turned.reshape(2, W, 4, T).astype(BF16)

        each(Z // 2, block)

    def send_z(p, source):
        for n, dx in enumerate(ORDER):
            first = ((x + dx) % X) * 8
            target = mid.at[p, pl.ds(first, 8), z]

            def one(dz):
                zt = (z + dz) % Z
                remote(source(zt, first), target, zs_sem.at[p], zr_sem.at[p, n], device(x, zt, yc)).start()

            all_of(Z, one, 1)
            pltpu.make_async_copy(source(z, first), target, local_sem.at[p, n]).start()

    def target_of(p):
        if p < CONVOLVED:
            return rcv.at[p, x, :, yc]
        return back.at[p - CONVOLVED, :, w]

    def forward(p, n):
        dx = ORDER[n]
        xt = (x + dx) % X
        part = mid.at[p, pl.ds(xt * 8, 8), z]
        pltpu.make_async_copy(part, part, local_sem.at[p, n]).wait()
        arrived = mid.at[p, pl.ds(xt * 8, 8), pl.ds(0, Z - 1)]
        remote(arrived, arrived, zs_sem.at[p], zr_sem.at[p, n], here).wait_recv()
        target = target_of(p)

        def one(i):
            there = (yc + i) % 8
            remote(mid.at[p, xt * 8 + there], target, xs_sem.at[p], xr_sem.at[p], device(xt, z, there)).start()

        all_of(8, one, 1 if dx == 0 else 0)
        if dx == 0:
            pltpu.make_async_copy(mid.at[p, w], target, local_sem.at[p, X]).start()

    def await_all(p):
        pltpu.make_async_copy(mid.at[p, w], target_of(p), local_sem.at[p, X]).wait()
        part = mid.at[p, pl.ds(0, W - 1)]
        remote(part, part, xs_sem.at[p], xr_sem.at[p], here).wait_recv()

    def send_scale(n):
        def one(dz):
            remote(
                own_scale.at[n], mid_scale.at[n, z], scale_zs_sem.at[n], scale_zr_sem.at[n],
                device(x, (z + dz) % Z, yc),
            ).start()

        all_of(Z, one, 1)
        pltpu.make_async_copy(own_scale.at[n], mid_scale.at[n, z], scale_local_sem.at[n, 0]).start()

    def scale_target(n):
        if n == IN_SCALES:
            return in_scale.at[x, :, yc]
        return out_scale.at[n - 1, :, w]

    def forward_scale(n):
        pltpu.make_async_copy(own_scale.at[n], mid_scale.at[n, z], scale_local_sem.at[n, 0]).wait()
        arrived = mid_scale.at[n, pl.ds(0, Z - 1)]
        remote(arrived, arrived, scale_zs_sem.at[n], scale_zr_sem.at[n], here).wait_recv()

        def one(i):
            there = (w + i) % W
            remote(
                mid_scale.at[n], scale_target(n), scale_xs_sem.at[n], scale_xr_sem.at[n],
                device(there // 8, z, there % 8),
            ).start()

        all_of(W, one, 1)
        pltpu.make_async_copy(mid_scale.at[n], scale_target(n), scale_local_sem.at[n, 1]).start()

    def await_scale(n):
        pltpu.make_async_copy(mid_scale.at[n], scale_target(n), scale_local_sem.at[n, 1]).wait()
        part = out_scale.at[0, :, pl.ds(0, W - 1)]
        remote(part, part, scale_xs_sem.at[n], scale_xr_sem.at[n], here).wait_recv()

    def in_send(p):
        send_z(p, lambda zt, first: snd.at[p, zt, pl.ds(first, 8)])

    loads[0].wait()
    pack(FILTER, lambda cols: encode(fin[:, cols], FILTER_TOP))
    for load in loads[1:5]:
        load.wait()
    pl.semaphore_wait(barrier, Z + W)
    streams = (qin, kin, vin)
    halos = [
        remote(stream.at[pl.ds(T - 16, 16)], before.at[n], halo_s_sem.at[n], halo_r_sem.at[n], next_device)
        for n, stream in enumerate(streams)
    ]

    @pl.when(d != D - 1)
    def _():
        for halo in halos:
            halo.start()

    in_send(FILTER)

    @pl.when(d != 0)
    def _():
        for halo in halos:
            halo.wait_recv()

    tops[...] = jnp.zeros(tops.shape, F32)

    def gate_block(b):
        cols = columns_of(b)
        for n, stream in enumerate(streams):
            extended[n, 0:8, cols] = before[n, :, cols].astype(F32)[8:16]
            extended[n, 8 : T + 8, cols] = stream[:, cols].astype(F32)
            short[n, :, cols] = (
                taps[n, 0:1, cols] * extended[n, 8 : T + 8, cols]
                + taps[n, 1:2, cols] * extended[n, 7 : T + 7, cols]
                + taps[n, 2:3, cols] * extended[n, 6 : T + 6, cols]
            )
        value = short[1, :, cols] * short[2, :, cols]
        gated[:, cols] = value
        tops[0] = jnp.maximum(tops[0], jnp.max(jnp.abs(value).reshape(16, 8, 256), axis=0))
        value = gin[:, cols].astype(F32) * short[0, :, cols]
        grad_mixed[:, cols] = value
        tops[1] = jnp.maximum(tops[1], jnp.max(jnp.abs(value).reshape(16, 8, 256), axis=0))

    each(4, gate_block)

    def top_of(n):
        return jnp.maximum(jnp.max(tops[n], keepdims=True), 1e-30)

    gated_top, grad_top = top_of(0), top_of(1)
    first_half = lax.broadcasted_iota(jnp.int32, (1, T), 1) < T // 2
    own_scale[IN_SCALES] = jnp.where(first_half, gated_top, grad_top)
    pack(GATED, lambda cols: encode(gated[:, cols], gated_top))
    send_scale(IN_SCALES)
    in_send(GATED)
    pack(GRAD_MIXED, lambda cols: encode(grad_mixed[:, cols], grad_top))
    in_send(GRAD_MIXED)
    for load in loads[5:]:
        load.wait()

    def unpack(p):
        await_all(p)
        for b in range(X):
            rows[pl.ds(b * 256, 256)] = rcv[p, b].astype(F32).reshape(256, T)

    def row(j):
        return rows[pl.ds(j, D, stride=4), :]

    def put_columns(v, at):
        high, low = halves_of(v)
        work[0, 0:D, pl.ds(at * T, T)] = high
        work[1, 0:D, pl.ds(at * T, T)] = low

    def transform(out, pair):
        for b in range(2):
            part = pl.ds(b * D, D)
            high = work[0, 0:D]
            coarse[part] = (
                dot(fwd[0, part], high) + dot(fwd[1, part], high) + dot(fwd[0, part], work[1, 0:D])
            )
        tc, ts = twist[0], twist[1]
        for n in range(2):
            cols = pl.ds(n * T, T)
            re, im = coarse[0:D, cols], coarse[D : 2 * D, cols]
            both = jnp.concatenate([re * tc + im * ts, im * tc - re * ts], axis=1)
            high, low = halves_of(both)
            out[2 * pair + n] = (
                dot(high, fine[0, 0]) + dot(low, fine[0, 0]) + dot(high, fine[0, 1])
            )

    def untransform(left, right, conjugate, out, pair):
        tc, ts = twist[0], twist[1]
        for n in range(2):
            a, b = left[2 * pair + n], right[2 * pair + n]
            ar, ai, br, bi = a[:, 0:T], a[:, T:], b[:, 0:T], b[:, T:]
            if conjugate:
                re, im = ar * br + ai * bi, ar * bi - ai * br
            else:
                re, im = ar * br - ai * bi, ar * bi + ai * br
            high, low = halves_of(jnp.concatenate([re, im], axis=1))
            back_spec = dot(high, fine[1, 0]) + dot(low, fine[1, 0]) + dot(high, fine[1, 1])
            gr, gi = back_spec[:, 0:T], back_spec[:, T:]
            cols = pl.ds(n * T, T)
            high, low = halves_of(gr * tc - gi * ts)
            work[0, 0:D, cols] = high
            work[1, 0:D, cols] = low
            high, low = halves_of(gi * tc + gr * ts)
            work[0, D : 2 * D, cols] = high
            work[1, D : 2 * D, cols] = low
        value = dot(bwd[0], work[0]) + dot(bwd[1], work[0]) + dot(bwd[0], work[1])
        for n in range(2):
            out[2 * pair + n] = value[:, n * T : n * T + T]

    def filter_pair(pair):
        for n in range(2):
            put_columns(decode(row(2 * pair + n), FILTER_TOP), n)
        transform(spec.at[0], pair)

    def convolve_pair(half, conjugate):
        def body(pair):
            top = jnp.broadcast_to(
                in_scale[...].reshape(D, T)[:, half * 64 : half * 64 + 1], (D, T)
            )
            for n in range(2):
                put_columns(decode(row(2 * pair + n), top), n)
            transform(spec.at[1], pair)
            untransform(spec.at[0], spec.at[1], conjugate, result, pair)

        return body

    def out_send(p):
        top = jnp.max(jnp.max(jnp.abs(result[...]), axis=0), keepdims=True)
        top = jnp.maximum(top, 1e-30)
        own_scale[p - CONVOLVED + 1] = jnp.broadcast_to(top, (1, T))

        def code_row(j):
            rows[pl.ds(j, D, stride=4), :] = encode(result[j], top)

        each(4, code_row)
        for b in range(X):
            osnd[p - CONVOLVED, pl.ds(b * 8, 8)] = (
                rows[pl.ds(b * 256, 256)].reshape(Z, 8, 4, T).swapaxes(0, 1).astype(BF16)
            )
        send_scale(p - CONVOLVED + 1)
        send_z(p, lambda zt, first: osnd.at[p - CONVOLVED, pl.ds(first, 8), zt])

    for n in range(X):
        forward(FILTER, n)
    forward_scale(IN_SCALES)
    unpack(FILTER)
    each(2, filter_pair)
    for n in range(X):
        forward(GATED, n)
    await_scale(IN_SCALES)
    unpack(GATED)
    conv = convolve_pair(0, False)
    conv(0)
    for n in range(X):
        forward(GRAD_MIXED, n)
    conv(1)
    out_send(CONVOLVED)
    unpack(GRAD_MIXED)
    each(2, convolve_pair(1, True))
    out_send(GRAD_GATED)
    forward_scale(CONVOLVED_SCALE)
    for n in range(X):
        forward(CONVOLVED, n)
    forward_scale(GRAD_SCALE)

    def make_scale_row(n):
        await_scale(n + 1)
        owner = lax.broadcasted_iota(jnp.int32, (D, 1024), 0)
        channel = lax.broadcasted_iota(jnp.int32, (D, 1024), 1)
        top = jnp.tile(out_scale[n].reshape(D, T), (1, 8))
        scale_row[n : n + 1] = jnp.sum(jnp.where(channel // 4 == owner, top, 0.0), axis=0, keepdims=True)

    def returned(n, b):
        cols = columns_of(b)
        code = lax.dot_general(
            back[n, pl.ds(b * 2, 2)].reshape(256, T), eye[...], (((0,), (0,)), ((), ())),
            preferred_element_type=F32,
        )
        return decode(code, scale_row[n : n + 1, cols])

    def backward_halo(n):
        return remote(
            extended.at[n, pl.ds(0, 8)], after.at[n], halo_s_sem.at[3 + n], halo_r_sem.at[3 + n], last_device
        )

    def send_halo(n):
        @pl.when(d != 0)
        def _():
            backward_halo(n).start()

    def await_halo(n):
        @pl.when(d != D - 1)
        def _():
            backward_halo(n).wait_recv()

    def mix_block(b):
        cols = columns_of(b)
        mixed = returned(0, b) + skip[:, cols] * gated[:, cols]
        held[0, :, cols] = (short[0, :, cols] * mixed).astype(BF16)
        extended[0, 0:T, cols] = gin[:, cols].astype(F32) * mixed

    def grad_block(b):
        cols = columns_of(b)
        total = returned(1, b) + skip[:, cols] * grad_mixed[:, cols]
        extended[1, 0:T, cols] = total * short[2, :, cols]
        extended[2, 0:T, cols] = total * short[1, :, cols]

    results = [
        pltpu.make_async_copy(held.at[n], ref, held_sem.at[n])
        for n, ref in enumerate((out_hbm, grad_q_hbm, grad_k_hbm, grad_v_hbm))
    ]

    def finish(n):
        def block(b):
            cols = columns_of(b)
            extended[n, T : T + 8, cols] = after[n, :, cols]
            held[n + 1, :, cols] = (
                taps[n, 0:1, cols] * extended[n, 0:T, cols]
                + taps[n, 1:2, cols] * extended[n, 1 : T + 1, cols]
                + taps[n, 2:3, cols] * extended[n, 2 : T + 2, cols]
            ).astype(BF16)

        each(4, block)
        results[n + 1].start()

    make_scale_row(0)
    await_all(CONVOLVED)
    each(4, mix_block)
    send_halo(0)
    results[0].start()
    for n in range(X):
        forward(GRAD_GATED, n)
    make_scale_row(1)
    await_all(GRAD_GATED)
    each(4, grad_block)
    send_halo(1)
    send_halo(2)
    await_halo(0)
    finish(0)
    await_halo(1)
    finish(1)
    await_halo(2)
    finish(2)

    @pl.when(d != D - 1)
    def _():
        for halo in halos:
            halo.wait_send()

    @pl.when(d != 0)
    def _():
        for n in range(3):
            backward_halo(n).wait_send()

    for copy in results:
        copy.wait()
    for p in range(5):
        sent = mid.at[p, pl.ds(0, W - 1)]
        remote(sent, sent, xs_sem.at[p], xr_sem.at[p], here).wait_send()
        sent = mid.at[p, :, pl.ds(0, Z - 1)]
        remote(sent, sent, zs_sem.at[p], zr_sem.at[p, 0], here).wait_send()
    for n in range(3):
        sent = out_scale.at[0, :, pl.ds(0, W - 1)]
        remote(sent, sent, scale_xs_sem.at[n], scale_xr_sem.at[n], here).wait_send()
        sent = mid_scale.at[n, pl.ds(0, Z - 1)]
        remote(sent, sent, scale_zs_sem.at[n], scale_zr_sem.at[n], here).wait_send()


def hand_on_kernel(*refs):
    ins, outs, (held, in_sem, out_sem) = refs[:4], refs[4:8], refs[8:]
    inward = [pltpu.make_async_copy(ins[n], held.at[n], in_sem.at[n]) for n in range(4)]
    outward = [pltpu.make_async_copy(held.at[n], outs[n], out_sem.at[n]) for n in range(4)]
    for copy in inward:
        copy.start()
    for n in range(4):
        inward[n].wait()
        outward[n].start()
    for copy in outward:
        copy.wait()


def local(query_in, key_in, value_in, conv_taps, long_filter, skip_gain, grad_out):
    forward, backward, fine, twist = (jnp.asarray(m) for m in dft_constants())
    anywhere = pl.BlockSpec(memory_space=pltpu.HBM)
    vmem = pl.BlockSpec(memory_space=pltpu.VMEM)
    tokens = pltpu.VMEM((T, 1024), BF16)
    wide = pltpu.VMEM((T, 1024), F32)
    result = jax.ShapeDtypeStruct((T, 1024), BF16)
    dma = pltpu.SemaphoreType.DMA
    outs = pl.pallas_call(
        main_kernel,
        out_shape=(result,) * 4,
        in_specs=[anywhere] * 5 + [vmem] * 2 + [anywhere] * 4,
        out_specs=(anywhere,) * 4,
        scratch_shapes=[
            tokens, tokens, tokens, tokens, wide,
            pltpu.VMEM(forward.shape, BF16),
            pltpu.VMEM(backward.shape, BF16),
            pltpu.VMEM(fine.shape, BF16),
            pltpu.VMEM(twist.shape, F32),
            pltpu.VMEM((256, 256), BF16),
            pltpu.VMEM((3, Z, W, 4, T), BF16),
            pltpu.VMEM((5, W, Z, 4, T), BF16),
            pltpu.VMEM((3, X, Z, 8, 4, T), BF16),
            pltpu.VMEM((4 * D, T), F32),
            pltpu.VMEM((2, 4, D, 2 * T), F32),
            pltpu.VMEM((2 * D, 2 * T), F32),
            pltpu.VMEM((2, 2 * D, 2 * T), BF16),
            pltpu.VMEM((4, D, T), F32),
            pltpu.VMEM((3, T + 8, 1024), F32),
            pltpu.VMEM((3, T, 1024), F32),
            wide, wide,
            pltpu.VMEM((2, 8, 256), F32),
            pltpu.VMEM((2, W, Z, 4, T), BF16),
            pltpu.VMEM((2, Z, W, 4, T), BF16),
            pltpu.VMEM((3, 16, 1024), BF16),
            pltpu.VMEM((3, 8, 1024), F32),
            pltpu.VMEM((3, 1, T), F32),
            pltpu.VMEM((3, Z, 1, T), F32),
            pltpu.VMEM((X, Z, 8, 1, T), F32),
            pltpu.VMEM((2, Z, W, 1, T), F32),
            pltpu.VMEM((2, 1024), F32),
            pltpu.VMEM((4, T, 1024), BF16),
            dma((9,)), dma((4,)), dma((5, X + 1)), dma((5,)), dma((5, X)), dma((5,)), dma((5,)),
            dma((6,)), dma((6,)),
            dma((3, 2)), dma((3,)), dma((3,)), dma((3,)), dma((3,)),
        ],
        compiler_params=pltpu.CompilerParams(
            collective_id=0, has_side_effects=True, vmem_limit_bytes=67043328
        ),
        name="hyena_exchange",
    )(
        query_in, key_in, value_in, grad_out, long_filter, conv_taps, skip_gain.reshape(1, 1024),
        forward, backward, fine, twist,
    )
    anyhow = pl.BlockSpec(memory_space=pltpu.HBM)
    return tuple(
        pl.pallas_call(
            hand_on_kernel,
            out_shape=(result,) * 4,
            in_specs=[anyhow] * 4,
            out_specs=(anyhow,) * 4,
            scratch_shapes=[pltpu.VMEM((4, T, 1024), BF16), dma((4,)), dma((4,))],
            compiler_params=pltpu.CompilerParams(vmem_limit_bytes=67043328),
            name="hyena_hand_on",
        )(*outs)
    )


def solution(mesh):
    tokens = P(("outer", "inner"), None)
    return jax.shard_map(
        local,
        mesh=mesh,
        in_specs=(tokens, tokens, tokens, P(), tokens, P(), tokens),
        out_specs=(tokens,) * 4,
        check_vma=False,
    )
```

```python
import functools

import jax
import jax.numpy as jnp
import numpy as np
from jax import lax
from jax.experimental import pallas as pl
from jax.experimental.pallas import tpu as pltpu
from jax.sharding import PartitionSpec as P

MESH = pl.DeviceIdType.MESH
F32, BF16 = jnp.float32, jnp.bfloat16
X, Z, Y, C = 4, 8, 4, 2
W = X * Y * C
D = 256
T = 128
POINTS = 2 * D * T


def dft_constants():
    k = np.arange(D)[:, None] + 0.5
    d = np.arange(D)[None, :]
    coarse = 2 * np.pi * (k * d / (2 * D) % 1.0)
    forward = np.concatenate([np.cos(coarse), -np.sin(coarse)], 0)
    backward = np.concatenate([np.cos(coarse).T, -np.sin(coarse).T], 1) * (2.0 / POINTS)
    t = np.arange(T)[None, :]
    turn = 2 * np.pi * (k * t / POINTS % 1.0)
    fine = 2 * np.pi * (t.T * t % T) / T
    c, s = np.cos(fine), np.sin(fine)
    fine_forward = np.block([[c, -s], [s, c]])
    fine_backward = np.block([[c, s], [-s, c]])

    def halves(m):
        m = m.astype(np.float32)
        high = m.astype(jnp.bfloat16)
        low = (m - high.astype(np.float32)).astype(jnp.bfloat16)
        return np.stack([high, low])

    fine_both = np.stack([halves(fine_forward), halves(fine_backward)])
    twist = np.stack([np.cos(turn), np.sin(turn)]).astype(np.float32)
    return halves(forward), halves(backward), fine_both, twist


def place():
    o, i = lax.axis_index("outer"), lax.axis_index("inner")
    return o // 4, (o % 4) * 2 + i // 8, i % 8


def device(x, z, yc):
    return (x * 4 + z // 2, (z % 2) * 8 + yc)


def halves_of(v):
    high = v.astype(BF16)
    return high, (v - high.astype(F32)).astype(BF16)


def dot(a, b):
    return jnp.dot(a, b, preferred_element_type=F32)


def identity():
    r = lax.broadcasted_iota(jnp.int32, (256, 256), 0)
    c = lax.broadcasted_iota(jnp.int32, (256, 256), 1)
    return jnp.where(r == c, 1.0, 0.0).astype(BF16)


FILTER, GATED, GRAD_MIXED, CONVOLVED, GRAD_GATED = range(5)
ORDER = (2, 1, 3, 0)
IN_SCALES, CONVOLVED_SCALE, GRAD_SCALE = range(3)

RATIO = 256.0
SHIFT = 124.0 * float(np.log(2.0))
SLOPE = 2.0 * SHIFT / float(np.log(1.0 + RATIO))
FILTER_TOP = 1.125


def encode(v, top):
    size = jnp.exp(SLOPE * jnp.log(1.0 + jnp.abs(v) * (RATIO / top)) - SHIFT)
    return jnp.where(v < 0.0, -size, size)


def decode(code, top):
    size = (jnp.exp((jnp.log(jnp.abs(code)) + SHIFT) * (1.0 / SLOPE)) - 1.0) * (top / RATIO)
    return jnp.where(code < 0.0, -size, size)


def main_kernel(
    q_hbm, k_hbm, v_hbm, g_hbm, f_hbm, taps, skip, fwd_hbm, bwd_hbm, fine_hbm, twist_hbm,
    out_hbm, grad_q_hbm, grad_k_hbm, grad_v_hbm,
    kin, vin, qin, gin, fin, fwd, bwd, fine, twist,
    eye, snd, mid, rcv, rows, spec, coarse, work, result, extended, short, gated, grad_mixed, tops,
    osnd, back, before, after, own_scale, mid_scale, in_scale, out_scale, scale_row, held,
    in_sem, held_sem, local_sem, zs_sem, zr_sem, xs_sem, xr_sem, halo_s_sem, halo_r_sem,
    scale_local_sem, scale_zs_sem, scale_zr_sem, scale_xs_sem, scale_xr_sem,
):
    x, z, yc = place()
    w = x * 8 + yc
    d = x * 64 + z * 8 + yc
    next_d, last_d = (d + 1) % D, (d + D - 1) % D
    next_device = device(next_d // 64, (next_d // 8) % 8, next_d % 8)
    last_device = device(last_d // 64, (last_d // 8) % 8, last_d % 8)
    here = device(x, z, yc)

    loads = [
        pltpu.make_async_copy(a, b, in_sem.at[n])
        for n, (a, b) in enumerate(
            [(f_hbm, fin), (k_hbm, kin), (v_hbm, vin), (q_hbm, qin), (g_hbm, gin),
             (fwd_hbm, fwd), (fine_hbm, fine), (twist_hbm, twist), (bwd_hbm, bwd)]
        )
    ]
    for load in loads:
        load.start()
    before[...] = jnp.zeros(before.shape, BF16)
    after[...] = jnp.zeros(after.shape, F32)

    barrier = pltpu.get_barrier_semaphore()

    def greet_z(i, _):
        pl.semaphore_signal(barrier, inc=1, device_id=device(x, (z + i) % Z, yc), device_id_type=MESH)
        return 0

    def greet_w(i, _):
        there = (w + i) % W
        pl.semaphore_signal(barrier, inc=1, device_id=device(there // 8, z, there % 8), device_id_type=MESH)
        return 0

    lax.fori_loop(1, Z, greet_z, 0)
    lax.fori_loop(1, W, greet_w, 0)
    for neighbour in (next_device, last_device):
        pl.semaphore_signal(barrier, inc=1, device_id=neighbour, device_id_type=MESH)
    eye[...] = identity()

    def remote(src, dst, send, recv, to):
        return pltpu.make_async_remote_copy(
            src_ref=src, dst_ref=dst, send_sem=send, recv_sem=recv, device_id=to, device_id_type=MESH
        )

    def each(count, body, first=0):
        def step(i, _):
            body(i)
            return 0

        lax.fori_loop(first, count, step, 0)

    def all_of(count, body, first=0):
        for i in range(first, count):
            body(i)

    def columns_of(b):
        return slice(b * 256, b * 256 + 256)

    def pack(p, code):
        def block(b):
            turned = lax.dot_general(
                eye[...], code(columns_of(b)).astype(BF16), (((1,), (1,)), ((), ())),
                preferred_element_type=F32,
            )
            snd[p, pl.ds(b * 2, 2)] = turned.reshape(2, W, 4, T).astype(BF16)

        all_of(Z // 2, block)

    def send_z(p, source):
        for n, dx in enumerate(ORDER):
            first = ((x + dx) % X) * 8
            target = mid.at[p, pl.ds(first, 8), z]

            def one(dz):
                zt = (z + dz) % Z
                remote(source(zt, first), target, zs_sem.at[p], zr_sem.at[p, n], device(x, zt, yc)).start()

            all_of(Z, one, 1)
            pltpu.make_async_copy(source(z, first), target, local_sem.at[p, n]).start()

    def target_of(p):
        if p < CONVOLVED:
            return rcv.at[p, x, :, yc]
        return back.at[p - CONVOLVED, :, w]

    def forward(p, n):
        dx = ORDER[n]
        xt = (x + dx) % X
        part = mid.at[p, pl.ds(xt * 8, 8), z]
        pltpu.make_async_copy(part, part, local_sem.at[p, n]).wait()
        arrived = mid.at[p, pl.ds(xt * 8, 8), pl.ds(0, Z - 1)]
        remote(arrived, arrived, zs_sem.at[p], zr_sem.at[p, n], here).wait_recv()
        target = target_of(p)

        def one(i):
            there = (yc + i) % 8
            remote(mid.at[p, xt * 8 + there], target, xs_sem.at[p], xr_sem.at[p], device(xt, z, there)).start()

        all_of(8, one, 1 if dx == 0 else 0)
        if dx == 0:
            pltpu.make_async_copy(mid.at[p, w], target, local_sem.at[p, X]).start()

    def await_all(p):
        pltpu.make_async_copy(mid.at[p, w], target_of(p), local_sem.at[p, X]).wait()
        part = mid.at[p, pl.ds(0, W - 1)]
        remote(part, part, xs_sem.at[p], xr_sem.at[p], here).wait_recv()

    def send_scale(n):
        def one(dz):
            remote(
                own_scale.at[n], mid_scale.at[n, z], scale_zs_sem.at[n], scale_zr_sem.at[n],
                device(x, (z + dz) % Z, yc),
            ).start()

        all_of(Z, one, 1)
        pltpu.make_async_copy(own_scale.at[n], mid_scale.at[n, z], scale_local_sem.at[n, 0]).start()

    def scale_target(n):
        if n == IN_SCALES:
            return in_scale.at[x, :, yc]
        return out_scale.at[n - 1, :, w]

    def forward_scale(n):
        pltpu.make_async_copy(own_scale.at[n], mid_scale.at[n, z], scale_local_sem.at[n, 0]).wait()
        arrived = mid_scale.at[n, pl.ds(0, Z - 1)]
        remote(arrived, arrived, scale_zs_sem.at[n], scale_zr_sem.at[n], here).wait_recv()

        def one(i):
            there = (w + i) % W
            remote(
                mid_scale.at[n], scale_target(n), scale_xs_sem.at[n], scale_xr_sem.at[n],
                device(there // 8, z, there % 8),
            ).start()

        all_of(W, one, 1)
        pltpu.make_async_copy(mid_scale.at[n], scale_target(n), scale_local_sem.at[n, 1]).start()

    def await_scale(n):
        pltpu.make_async_copy(mid_scale.at[n], scale_target(n), scale_local_sem.at[n, 1]).wait()
        part = out_scale.at[0, :, pl.ds(0, W - 1)]
        remote(part, part, scale_xs_sem.at[n], scale_xr_sem.at[n], here).wait_recv()

    def in_send(p):
        send_z(p, lambda zt, first: snd.at[p, zt, pl.ds(first, 8)])

    loads[0].wait()
    pack(FILTER, lambda cols: encode(fin[:, cols], FILTER_TOP))
    for load in loads[1:5]:
        load.wait()
    pl.semaphore_wait(barrier, Z + W)
    streams = (qin, kin, vin)
    halos = [
        remote(stream.at[pl.ds(T - 16, 16)], before.at[n], halo_s_sem.at[n], halo_r_sem.at[n], next_device)
        for n, stream in enumerate(streams)
    ]

    @pl.when(d != D - 1)
    def _():
        for halo in halos:
            halo.start()

    in_send(FILTER)

    @pl.when(d != 0)
    def _():
        for halo in halos:
            halo.wait_recv()

    tops[...] = jnp.zeros(tops.shape, F32)

    def gate_block(b):
        cols = columns_of(b)
        for n, stream in enumerate(streams):
            extended[n, 0:8, cols] = before[n, :, cols].astype(F32)[8:16]
            extended[n, 8 : T + 8, cols] = stream[:, cols].astype(F32)
            short[n, :, cols] = (
                taps[n, 0:1, cols] * extended[n, 8 : T + 8, cols]
                + taps[n, 1:2, cols] * extended[n, 7 : T + 7, cols]
                + taps[n, 2:3, cols] * extended[n, 6 : T + 6, cols]
            )
        value = short[1, :, cols] * short[2, :, cols]
        gated[:, cols] = value
        tops[0] = jnp.maximum(tops[0], jnp.max(jnp.abs(value).reshape(16, 8, 256), axis=0))
        value = gin[:, cols].astype(F32) * short[0, :, cols]
        grad_mixed[:, cols] = value
        tops[1] = jnp.maximum(tops[1], jnp.max(jnp.abs(value).reshape(16, 8, 256), axis=0))

    all_of(4, gate_block)

    def top_of(n):
        return jnp.maximum(jnp.max(tops[n], keepdims=True), 1e-30)

    gated_top, grad_top = top_of(0), top_of(1)
    first_half = lax.broadcasted_iota(jnp.int32, (1, T), 1) < T // 2
    own_scale[IN_SCALES] = jnp.where(first_half, gated_top, grad_top)
    pack(GATED, lambda cols: encode(gated[:, cols], gated_top))
    send_scale(IN_SCALES)
    in_send(GATED)
    pack(GRAD_MIXED, lambda cols: encode(grad_mixed[:, cols], grad_top))
    in_send(GRAD_MIXED)
    for load in loads[5:]:
        load.wait()

    def unpack(p):
        await_all(p)
        for b in range(X):
            rows[pl.ds(b * 256, 256)] = rcv[p, b].astype(F32).reshape(256, T)

    def row(j):
        return rows[pl.ds(j, D, stride=4), :]

    def put_columns(v, at):
        high, low = halves_of(v)
        work[0, 0:D, pl.ds(at * T, T)] = high
        work[1, 0:D, pl.ds(at * T, T)] = low

    def transform(out, pair):
        for b in range(2):
            part = pl.ds(b * D, D)
            high = work[0, 0:D]
            coarse[part] = (
                dot(fwd[0, part], high) + dot(fwd[1, part], high) + dot(fwd[0, part], work[1, 0:D])
            )
        tc, ts = twist[0], twist[1]
        for n in range(2):
            cols = pl.ds(n * T, T)
            re, im = coarse[0:D, cols], coarse[D : 2 * D, cols]
            both = jnp.concatenate([re * tc + im * ts, im * tc - re * ts], axis=1)
            high, low = halves_of(both)
            out[2 * pair + n] = (
                dot(high, fine[0, 0]) + dot(low, fine[0, 0]) + dot(high, fine[0, 1])
            )

    def untransform(left, right, conjugate, out, pair):
        tc, ts = twist[0], twist[1]
        for n in range(2):
            a, b = left[2 * pair + n], right[2 * pair + n]
            ar, ai, br, bi = a[:, 0:T], a[:, T:], b[:, 0:T], b[:, T:]
            if conjugate:
                re, im = ar * br + ai * bi, ar * bi - ai * br
            else:
                re, im = ar * br - ai * bi, ar * bi + ai * br
            high, low = halves_of(jnp.concatenate([re, im], axis=1))
            back_spec = dot(high, fine[1, 0]) + dot(low, fine[1, 0]) + dot(high, fine[1, 1])
            gr, gi = back_spec[:, 0:T], back_spec[:, T:]
            cols = pl.ds(n * T, T)
            high, low = halves_of(gr * tc - gi * ts)
            work[0, 0:D, cols] = high
            work[1, 0:D, cols] = low
            high, low = halves_of(gi * tc + gr * ts)
            work[0, D : 2 * D, cols] = high
            work[1, D : 2 * D, cols] = low
        value = dot(bwd[0], work[0]) + dot(bwd[1], work[0]) + dot(bwd[0], work[1])
        for n in range(2):
            out[2 * pair + n] = value[:, n * T : n * T + T]

    def filter_pair(pair):
        for n in range(2):
            put_columns(decode(row(2 * pair + n), FILTER_TOP), n)
        transform(spec.at[0], pair)

    def convolve_pair(half, conjugate):
        def body(pair):
            top = jnp.broadcast_to(
                in_scale[...].reshape(D, T)[:, half * 64 : half * 64 + 1], (D, T)
            )
            for n in range(2):
                put_columns(decode(row(2 * pair + n), top), n)
            transform(spec.at[1], pair)
            untransform(spec.at[0], spec.at[1], conjugate, result, pair)

        return body

    def out_send(p):
        top = jnp.max(jnp.max(jnp.abs(result[...]), axis=0), keepdims=True)
        top = jnp.maximum(top, 1e-30)
        own_scale[p - CONVOLVED + 1] = jnp.broadcast_to(top, (1, T))

        def code_row(j):
            rows[pl.ds(j, D, stride=4), :] = encode(result[j], top)

        each(4, code_row)
        for b in range(X):
            osnd[p - CONVOLVED, pl.ds(b * 8, 8)] = (
                rows[pl.ds(b * 256, 256)].reshape(Z, 8, 4, T).swapaxes(0, 1).astype(BF16)
            )
        send_scale(p - CONVOLVED + 1)
        send_z(p, lambda zt, first: osnd.at[p - CONVOLVED, pl.ds(first, 8), zt])

    for n in range(X):
        forward(FILTER, n)
    forward_scale(IN_SCALES)
    unpack(FILTER)
    each(2, filter_pair)
    for n in range(X):
        forward(GATED, n)
    await_scale(IN_SCALES)
    unpack(GATED)
    conv = convolve_pair(0, False)
    conv(0)
    for n in range(X):
        forward(GRAD_MIXED, n)
    conv(1)
    out_send(CONVOLVED)
    unpack(GRAD_MIXED)
    each(2, convolve_pair(1, True))
    out_send(GRAD_GATED)
    forward_scale(CONVOLVED_SCALE)
    for n in range(X):
        forward(CONVOLVED, n)
    forward_scale(GRAD_SCALE)

    def make_scale_row(n):
        await_scale(n + 1)
        owner = lax.broadcasted_iota(jnp.int32, (D, 1024), 0)
        channel = lax.broadcasted_iota(jnp.int32, (D, 1024), 1)
        top = jnp.tile(out_scale[n].reshape(D, T), (1, 8))
        scale_row[n : n + 1] = jnp.sum(jnp.where(channel // 4 == owner, top, 0.0), axis=0, keepdims=True)

    def returned(n, b):
        cols = columns_of(b)
        code = lax.dot_general(
            back[n, pl.ds(b * 2, 2)].reshape(256, T), eye[...], (((0,), (0,)), ((), ())),
            preferred_element_type=F32,
        )
        return decode(code, scale_row[n : n + 1, cols])

    def backward_halo(n):
        return remote(
            extended.at[n, pl.ds(0, 8)], after.at[n], halo_s_sem.at[3 + n], halo_r_sem.at[3 + n], last_device
        )

    def send_halo(n):
        @pl.when(d != 0)
        def _():
            backward_halo(n).start()

    def await_halo(n):
        @pl.when(d != D - 1)
        def _():
            backward_halo(n).wait_recv()

    def mix_block(b):
        cols = columns_of(b)
        mixed = returned(0, b) + skip[:, cols] * gated[:, cols]
        held[0, :, cols] = (short[0, :, cols] * mixed).astype(BF16)
        extended[0, 0:T, cols] = gin[:, cols].astype(F32) * mixed

    def grad_block(b):
        cols = columns_of(b)
        total = returned(1, b) + skip[:, cols] * grad_mixed[:, cols]
        extended[1, 0:T, cols] = total * short[2, :, cols]
        extended[2, 0:T, cols] = total * short[1, :, cols]

    results = [
        pltpu.make_async_copy(held.at[n], ref, held_sem.at[n])
        for n, ref in enumerate((out_hbm, grad_q_hbm, grad_k_hbm, grad_v_hbm))
    ]

    def finish(n):
        def block(b):
            cols = columns_of(b)
            extended[n, T : T + 8, cols] = after[n, :, cols]
            held[n + 1, :, cols] = (
                taps[n, 0:1, cols] * extended[n, 0:T, cols]
                + taps[n, 1:2, cols] * extended[n, 1 : T + 1, cols]
                + taps[n, 2:3, cols] * extended[n, 2 : T + 2, cols]
            ).astype(BF16)

        all_of(4, block)
        results[n + 1].start()

    make_scale_row(0)
    await_all(CONVOLVED)
    all_of(4, mix_block)
    send_halo(0)
    results[0].start()
    for n in range(X):
        forward(GRAD_GATED, n)
    make_scale_row(1)
    await_all(GRAD_GATED)
    all_of(4, grad_block)
    send_halo(1)
    send_halo(2)
    await_halo(0)
    finish(0)
    await_halo(1)
    finish(1)
    await_halo(2)
    finish(2)

    @pl.when(d != D - 1)
    def _():
        for halo in halos:
            halo.wait_send()

    @pl.when(d != 0)
    def _():
        for n in range(3):
            backward_halo(n).wait_send()

    for copy in results:
        copy.wait()
    for p in range(5):
        sent = mid.at[p, pl.ds(0, W - 1)]
        remote(sent, sent, xs_sem.at[p], xr_sem.at[p], here).wait_send()
        sent = mid.at[p, :, pl.ds(0, Z - 1)]
        remote(sent, sent, zs_sem.at[p], zr_sem.at[p, 0], here).wait_send()
    for n in range(3):
        sent = out_scale.at[0, :, pl.ds(0, W - 1)]
        remote(sent, sent, scale_xs_sem.at[n], scale_xr_sem.at[n], here).wait_send()
        sent = mid_scale.at[n, pl.ds(0, Z - 1)]
        remote(sent, sent, scale_zs_sem.at[n], scale_zr_sem.at[n], here).wait_send()


def hand_on_kernel(*refs):
    ins, outs, (held, in_sem, out_sem) = refs[:4], refs[4:8], refs[8:]
    inward = [pltpu.make_async_copy(ins[n], held.at[n], in_sem.at[n]) for n in range(4)]
    outward = [pltpu.make_async_copy(held.at[n], outs[n], out_sem.at[n]) for n in range(4)]
    for copy in inward:
        copy.start()
    for n in range(4):
        inward[n].wait()
        outward[n].start()
    for copy in outward:
        copy.wait()


def local(query_in, key_in, value_in, conv_taps, long_filter, skip_gain, grad_out):
    forward, backward, fine, twist = (jnp.asarray(m) for m in dft_constants())
    anywhere = pl.BlockSpec(memory_space=pltpu.HBM)
    vmem = pl.BlockSpec(memory_space=pltpu.VMEM)
    tokens = pltpu.VMEM((T, 1024), BF16)
    wide = pltpu.VMEM((T, 1024), F32)
    result = jax.ShapeDtypeStruct((T, 1024), BF16)
    dma = pltpu.SemaphoreType.DMA
    outs = pl.pallas_call(
        main_kernel,
        out_shape=(result,) * 4,
        in_specs=[anywhere] * 5 + [vmem] * 2 + [anywhere] * 4,
        out_specs=(anywhere,) * 4,
        scratch_shapes=[
            tokens, tokens, tokens, tokens, wide,
            pltpu.VMEM(forward.shape, BF16),
            pltpu.VMEM(backward.shape, BF16),
            pltpu.VMEM(fine.shape, BF16),
            pltpu.VMEM(twist.shape, F32),
            pltpu.VMEM((256, 256), BF16),
            pltpu.VMEM((3, Z, W, 4, T), BF16),
            pltpu.VMEM((5, W, Z, 4, T), BF16),
            pltpu.VMEM((3, X, Z, 8, 4, T), BF16),
            pltpu.VMEM((4 * D, T), F32),
            pltpu.VMEM((2, 4, D, 2 * T), F32),
            pltpu.VMEM((2 * D, 2 * T), F32),
            pltpu.VMEM((2, 2 * D, 2 * T), BF16),
            pltpu.VMEM((4, D, T), F32),
            pltpu.VMEM((3, T + 8, 1024), F32),
            pltpu.VMEM((3, T, 1024), F32),
            wide, wide,
            pltpu.VMEM((2, 8, 256), F32),
            pltpu.VMEM((2, W, Z, 4, T), BF16),
            pltpu.VMEM((2, Z, W, 4, T), BF16),
            pltpu.VMEM((3, 16, 1024), BF16),
            pltpu.VMEM((3, 8, 1024), F32),
            pltpu.VMEM((3, 1, T), F32),
            pltpu.VMEM((3, Z, 1, T), F32),
            pltpu.VMEM((X, Z, 8, 1, T), F32),
            pltpu.VMEM((2, Z, W, 1, T), F32),
            pltpu.VMEM((2, 1024), F32),
            pltpu.VMEM((4, T, 1024), BF16),
            dma((9,)), dma((4,)), dma((5, X + 1)), dma((5,)), dma((5, X)), dma((5,)), dma((5,)),
            dma((6,)), dma((6,)),
            dma((3, 2)), dma((3,)), dma((3,)), dma((3,)), dma((3,)),
        ],
        compiler_params=pltpu.CompilerParams(
            collective_id=0, has_side_effects=True, vmem_limit_bytes=67043328
        ),
        name="hyena_exchange",
    )(
        query_in, key_in, value_in, grad_out, long_filter, conv_taps, skip_gain.reshape(1, 1024),
        forward, backward, fine, twist,
    )
    anyhow = pl.BlockSpec(memory_space=pltpu.HBM)
    return tuple(
        pl.pallas_call(
            hand_on_kernel,
            out_shape=(result,) * 4,
            in_specs=[anyhow] * 4,
            out_specs=(anyhow,) * 4,
            scratch_shapes=[pltpu.VMEM((4, T, 1024), BF16), dma((4,)), dma((4,))],
            compiler_params=pltpu.CompilerParams(vmem_limit_bytes=67043328),
            name="hyena_hand_on",
        )(*outs)
    )


def solution(mesh):
    tokens = P(("outer", "inner"), None)
    return jax.shard_map(
        local,
        mesh=mesh,
        in_specs=(tokens, tokens, tokens, P(), tokens, P(), tokens),
        out_specs=(tokens,) * 4,
        check_vma=False,
    )
```
